256 devices in a mesh: seq: 64 (over z, y, core), grp: 4 (over x).
Axes of the slice: x: 4, y: 4, z: 8, core: 2. Of those that a mesh axis runs over, the one named last changes fastest.
Arguments:
- q_nope: bfloat16 [1024, 128, 128], P('seq', 'grp'), may hold values from -6 to 6
- q_rope: bfloat16 [1024, 128, 64], P('seq', 'grp'), may hold values from -256 to 256
- cache: bfloat16 [65536, 576], P('seq'), may hold values from -6 to 6
- w_uk: bfloat16 [128, 65536], P('grp', 'seq'), may hold values from -0.5 to 0.5
- w_uv: bfloat16 [128, 65536], P('grp', 'seq'), may hold values from -0.25 to 0.25
- d_out: bfloat16 [1024, 128, 128], P('seq', 'grp'), may hold values from -6 to 6
- sel: int32 [1024, 32], P('seq'), may hold values from 0 to 63, as said below
- slot_blocks: int32 [64, 64], P('seq'), may hold values from 0 to 15, as said below
Outputs:
- attn_out: bfloat16 [1024, 128, 128], P('seq', 'grp')
- d_q_nope: bfloat16 [1024, 128, 128], P('seq', 'grp')
- d_q_rope: bfloat16 [1024, 128, 64], P('seq', 'grp')
- d_cache: float32 [65536, 576], P('seq')
The draws below stay inside these ranges and needn't reach their ends.
Inputs may be any that keep to these rules, and one draw needn't show every extreme that they name: `sel`: each row names 32 different places; place s stands for the block that the row's device asks of device s. `slot_blocks`: entry [r, s] is the index among device s's own blocks of the block that device r asks for in place s; the 1 entries of a row toward one device differ.
All inputs are finite; a program needn't handle non-finite values.
Results may differ from the reference program's by a relative error of at most 0.015.
Values may be sent and summed in bfloat16 or wider, within the bound.
A program may use at most 128 MiB of HBM per device.

```python
import math
import jax
import jax.numpy as jnp
from jax import lax

NUM_HEADS = 128
NOPE_DIM = 128
ROPE_DIM = 64
LATENT = 512
VALUE_DIM = 128
BLOCK_LEN = 64
PICKED = 32
SLOT_COUNT = 64
QUERY_DEV = 16
QUERIES = 1024
CONTEXT = 65536
PER_PEER = 1
DEV_BLOCKS = 16


def pick_slots(key):
    base = jax.random.fold_in(key, 11)
    scores = jax.random.randint(base, (QUERIES, SLOT_COUNT), 0, 2 ** 20) * SLOT_COUNT
    scores = scores + jnp.arange(SLOT_COUNT, dtype=jnp.int32)[None, :]
    scores = scores.at[0, SLOT_COUNT - 1].set(-2)
    scores = scores.at[0, 0].set(-1)
    order = jnp.argsort(scores, axis=1)
    return order[:, :PICKED].astype(jnp.int32)


def pick_blocks(key):
    peers = QUERIES // QUERY_DEV
    base = jax.random.fold_in(key, 12)
    scores = jax.random.randint(base, (peers, peers, DEV_BLOCKS), 0, 2 ** 20) * DEV_BLOCKS
    scores = scores + jnp.arange(DEV_BLOCKS, dtype=jnp.int32)[None, None, :]
    scores = scores.at[0, 0, DEV_BLOCKS - 1].set(-1)
    scores = scores.at[0, 1, 0].set(-1)
    order = jnp.argsort(scores, axis=2)
    return order[:, :, :PER_PEER].reshape(peers, SLOT_COUNT).astype(jnp.int32)


def draw_sel(key, part):
    return pick_slots(key)


def draw_slot_blocks(key, part):
    return pick_blocks(key)


def draw_cache(key, part):
    whole = jnp.clip(jax.random.normal(jax.random.fold_in(key, 15), (CONTEXT, LATENT + ROPE_DIM), jnp.float32), -6.0, 6.0)
    return whole.astype(jnp.bfloat16)


def draw_q_rope(key, part):
    drawn = jnp.clip(jax.random.normal(jax.random.fold_in(key, 16), (QUERIES, NUM_HEADS, ROPE_DIM), jnp.float32), -6.0, 6.0)
    return drawn.astype(jnp.bfloat16)


def steps_of(rng, shape, pieces, smallest, largest):
    factor_of, own = 1.0, jax.random.fold_in(rng, 6)
    for axis_at, shards_of in pieces:
        heights = jnp.exp(jax.random.uniform(jax.random.fold_in(own, axis_at), (shards_of,), jnp.float32, smallest / len(pieces), largest / len(pieces)))
        factor_of = factor_of * jnp.repeat(heights, shape[axis_at] // shards_of).reshape([-1 if axis == axis_at else 1 for axis in range(len(shape))])
    return factor_of


def centred(stream_key, extent, width, limit, cuts=(), kind=jnp.bfloat16):
    factor_of = steps_of(stream_key, extent, cuts, -0.22, 0.18) if cuts else 1.0
    entries = jax.random.normal(stream_key, extent, jnp.float32) * width * factor_of
    return jnp.minimum(jnp.maximum(entries, -limit), limit).astype(kind)


def setup_inputs(seed: int = 0) -> dict:
    splits = jax.random.split(jax.random.key(seed), 9)
    q_nope = centred(splits[0], (QUERIES, NUM_HEADS, NOPE_DIM), 1.0, 6.0, ((0, 64), (1, 4)))
    q_rope = draw_q_rope(jax.random.fold_in(splits[8], 71), 0)
    cache = draw_cache(jax.random.fold_in(splits[8], 71), 0)
    w_uk = centred(splits[3], (NUM_HEADS, NOPE_DIM * LATENT), NOPE_DIM ** -0.5, 0.5, ((0, 4), (1, 64)))
    w_uv = centred(splits[4], (NUM_HEADS, LATENT * VALUE_DIM), LATENT ** -0.5, 0.25, ((0, 4), (1, 64)))
    d_out = centred(splits[5], (QUERIES, NUM_HEADS, VALUE_DIM), 1.0, 6.0, ((0, 64), (1, 4)))
    sel = draw_sel(jax.random.fold_in(splits[8], 71), 0)
    slot_blocks = draw_slot_blocks(jax.random.fold_in(splits[8], 71), 0)
    return {"q_nope": q_nope, "q_rope": q_rope, "cache": cache, "w_uk": w_uk, "w_uv": w_uv, "d_out": d_out, "sel": sel, "slot_blocks": slot_blocks}


def reference(q_nope, q_rope, cache, w_uk, w_uv, d_out, sel, slot_blocks):
    scale = 1.0 / math.sqrt(NOPE_DIM + ROPE_DIM)
    weight_k = w_uk.reshape(NUM_HEADS, NOPE_DIM, LATENT).astype(jnp.float32)
    weight_v = w_uv.reshape(NUM_HEADS, LATENT, VALUE_DIM).astype(jnp.float32)
    q_lat = jnp.einsum('qhn,hnl->qhl', q_nope.astype(jnp.float32), weight_k).astype(jnp.bfloat16)
    qfull = jnp.concatenate([q_lat, q_rope], axis=-1)
    d_olat = jnp.einsum('qhv,hlv->qhl', d_out.astype(jnp.float32), weight_v).astype(jnp.bfloat16)
    offsets = jnp.arange(BLOCK_LEN, dtype=jnp.int32)

    def one_query(grads, item):
        query_full, query_dol, picks, row = item
        owner = (picks // PER_PEER).astype(jnp.int32)
        requester = (row // QUERY_DEV).astype(jnp.int32)
        inner = slot_blocks[requester][picks].astype(jnp.int32)
        block = owner * DEV_BLOCKS + inner
        tokens = (block[:, None] * BLOCK_LEN + offsets[None, :]).reshape(-1).astype(jnp.int32)
        keys = cache[tokens]
        keys_lat = keys[:, :LATENT]
        score = jnp.dot(query_full, keys.T, preferred_element_type=jnp.float32) * scale
        prob = jax.nn.softmax(score, axis=-1)
        prob_low = prob.astype(jnp.bfloat16)
        olat = jnp.dot(prob_low, keys_lat, preferred_element_type=jnp.float32).astype(jnp.bfloat16)
        dprob = jnp.dot(query_dol, keys_lat.T, preferred_element_type=jnp.float32)
        delta = lax.optimization_barrier(jnp.sum(prob * dprob, axis=-1, keepdims=True))
        dscore = (prob * (dprob - delta) * scale).astype(jnp.bfloat16)
        dquery = jnp.dot(dscore, keys, preferred_element_type=jnp.float32)
        value_part = jnp.dot(prob_low.T, query_dol, preferred_element_type=jnp.float32)
        dkeys = jnp.dot(dscore.T, query_full, preferred_element_type=jnp.float32)
        dkeys = dkeys + jnp.pad(value_part, ((0, 0), (0, ROPE_DIM)))
        grads = grads.at[tokens].add(dkeys)
        return (grads, (olat, dquery[:, :LATENT].astype(jnp.bfloat16), dquery[:, LATENT:].astype(jnp.bfloat16)))
    start = jnp.zeros((CONTEXT, LATENT + ROPE_DIM), jnp.float32)
    rows = jnp.arange(QUERIES, dtype=jnp.int32)
    d_cache, outs = lax.scan(one_query, start, (qfull, d_olat, sel, rows))
    olat, d_qlat, d_q_rope = outs
    attn_out = jnp.einsum('qhl,hlv->qhv', olat.astype(jnp.float32), weight_v).astype(jnp.bfloat16)
    d_q_nope = jnp.einsum('qhl,hnl->qhn', d_qlat.astype(jnp.float32), weight_k).astype(jnp.bfloat16)
    return (attn_out, d_q_nope, d_q_rope, d_cache)
```

```python
import math

import jax
import jax.numpy as jnp
from jax import lax
from jax.experimental import pallas as pl
from jax.experimental.pallas import tpu as pltpu
from jax.sharding import PartitionSpec as P

MESH = pl.DeviceIdType.MESH
BF = jnp.bfloat16
F32 = jnp.float32
ZN, YN, XN = 8, 4, 4
ORDER = (0, 1, 7, 2, 6, 3, 5, 4)
NEG = -1e30


def rcopy(src, dst, ssem, rsem, seq, grp):
    return pltpu.make_async_remote_copy(
        src_ref=src, dst_ref=dst, send_sem=ssem, recv_sem=rsem,
        device_id=(seq, grp), device_id_type=MESH,
    )


def place():
    si = lax.axis_index("seq")
    g = lax.axis_index("grp")
    c = lax.rem(si, 2)
    y = lax.rem(si // 2, YN)
    z = si // (2 * YN)
    return si, g, z, y, c


def sid(z, y, c):
    return (lax.rem(z, ZN) * YN + lax.rem(y, YN)) * 2 + c


def peers():
    return [(dz, dy, dc) for dz in ORDER for dy in range(YN) for dc in range(2) if (dz, dy, dc) != (0, 0, 0)]


def fetch_kernel(wsh, cache, slot, keys, wall, m_ref,
                 table, send, zs, zr, ys, yr, ss, sr, ixs, ixr, as_, ar, xs, xr, loc):
    si, g, z, y, c = place()
    zp, zm = sid(z + 1, y, c), sid(z + 7, y, c)
    yp, ym = sid(z, y + 1, c), sid(z, y + 3, c)
    sib = sid(z, y, 1 - c)
    gr, gl = lax.rem(g + 1, XN), lax.rem(g + 3, XN)
    sends = []

    def go(cp):
        cp.start()
        sends.append(cp)

    def src_of(a, b):
        return sid(z + (ZN - a), y + (YN - b), c)

    def half(ref, h):
        return ref.at[pl.ds(32 * h, 32)]

    own = pltpu.make_async_copy(wsh, wall.at[si], loc.at[0])
    own.start()
    mine = pltpu.make_async_copy(slot, table.at[si], loc.at[1])
    mine.start()
    for (dz, dy, dc) in peers():
        to = sid(z + dz, y + dy, lax.rem(c + dc, 2))
        go(rcopy(slot, table.at[si], ixs.at[dz, dy, dc], ixr.at[dz, dy, dc], to, g))
    go(rcopy(wsh, wall.at[si], zs.at[0, 0], zr.at[0, 0], zp, g))
    go(rcopy(wsh, wall.at[si], zs.at[1, 0], zr.at[1, 0], zm, g))

    def y_send(a):
        s = src_of(a, 0)
        ref = wsh if a == 0 else wall.at[s]
        go(rcopy(ref, wall.at[s], ys.at[a, 0, 0], yr.at[a, 0, 0], yp, g))
        go(rcopy(ref, wall.at[s], ys.at[a, 1, 0], yr.at[a, 1, 0], ym, g))
        go(rcopy(ref, wall.at[s], ss.at[a, 0], sr.at[a, 0], sib, g))

    def z_step(k):
        for d in range(2):
            a = k if d == 0 else ZN - k
            s = src_of(a, 0)
            ref = wall.at[s] if k < 4 else half(wall.at[s], d)
            to = zp if d == 0 else zm
            rcopy(ref, ref, zs.at[d, k - 1], zr.at[d, k - 1], to, g).wait_recv()
            if k < 4:
                nxt = wall.at[s] if k < 3 else half(wall.at[s], d)
                go(rcopy(nxt, nxt, zs.at[d, k], zr.at[d, k], to, g))

    def y_near(a):
        for d in range(2):
            s = src_of(a, 1 if d == 0 else 3)
            ref = wall.at[s]
            to = yp if d == 0 else ym
            rcopy(ref, ref, ys.at[a, d, 0], yr.at[a, d, 0], to, g).wait_recv()
            h = half(ref, d)
            go(rcopy(h, h, ys.at[a, d, 1], yr.at[a, d, 1], to, g))
            b = 1 if d == 0 else 3
            go(rcopy(ref, ref, ss.at[a, b], sr.at[a, b], sib, g))

    def y_far(a):
        s = src_of(a, 2)
        for d in range(2):
            h = half(wall.at[s], d)
            rcopy(h, h, ys.at[a, d, 1], yr.at[a, d, 1], yp if d == 0 else ym, g).wait_recv()
        go(rcopy(wall.at[s], wall.at[s], ss.at[a, 2], sr.at[a, 2], sib, g))

    y_send(0)
    z_step(1)
    y_send(1)
    y_send(7)
    mine.wait()
    for (dz, dy, dc) in peers():
        s = sid(z + (ZN - dz), y + (YN - dy), lax.rem(c + dc, 2))
        rcopy(slot, table.at[s], ixs.at[dz, dy, dc], ixr.at[dz, dy, dc], s, g).wait_recv()

    lane = lax.broadcasted_iota(jnp.int32, (8, 128), 1)
    col = lax.broadcasted_iota(jnp.int32, (8, 256), 1)
    row = lax.broadcasted_iota(jnp.int32, (8, 256), 0)
    colb, colt = col // 16, lax.rem(col, 16)

    def build(r, carry):
        v = jnp.sum(jnp.where(lane == si, table[r], 0), axis=1, keepdims=True)
        top = jnp.where((colb == v) & (colt == row), 1.0, 0.0)
        bot = jnp.where((colb == v) & (colt == row + 8), 1.0, 0.0)
        m_ref[r] = jnp.concatenate([top, bot], axis=0).astype(BF)
        return carry

    lax.fori_loop(0, 64, build, 0)
    cq = cache[:, g].reshape(256, 576)

    def pick(i, carry):
        rows = pl.ds(8 * i, 8)
        got = jnp.dot(m_ref[rows].reshape(128, 256), cq, preferred_element_type=F32)
        send[rows] = got.astype(BF).reshape(8, 16, 576)
        return carry

    lax.fori_loop(0, 8, pick, 0)
    z_step(2)
    y_send(2)
    y_send(6)
    keys[si, g] = send[si]
    for (dz, dy, dc) in peers():
        to = sid(z + dz, y + dy, lax.rem(c + dc, 2))
        go(rcopy(send.at[to], keys.at[si, g], as_.at[dz, dy, dc], ar.at[dz, dy, dc], to, g))
    z_step(3)
    y_send(3)
    y_send(5)
    z_step(4)
    y_send(4)

    def x_part(i, who, d, far):
        base = 8 * lax.rem(z + ZN - i, ZN)
        if far:
            return keys.at[pl.ds(base + 4 * d, 4), who]
        return keys.at[pl.ds(base, 8), who]

    def x_start(i):
        for dy in range(YN):
            for dc in range(2):
                if (i, dy, dc) != (0, 0, 0):
                    s = sid(z + (ZN - i), y + (YN - dy), lax.rem(c + dc, 2))
                    rcopy(send.at[s], keys.at[s, g], as_.at[i, dy, dc], ar.at[i, dy, dc], s, g).wait_recv()
        ref = x_part(i, g, 0, False)
        go(rcopy(ref, ref, xs.at[i, 0, 0], xr.at[i, 0, 0], si, gr))
        go(rcopy(ref, ref, xs.at[i, 1, 0], xr.at[i, 1, 0], si, gl))

    def x_fwd(i):
        for d in range(2):
            who = gl if d == 0 else gr
            to = gr if d == 0 else gl
            ref = x_part(i, who, d, False)
            rcopy(ref, ref, xs.at[i, d, 0], xr.at[i, d, 0], si, to).wait_recv()
            h = x_part(i, who, d, True)
            go(rcopy(h, h, xs.at[i, d, 1], xr.at[i, d, 1], si, to))

    def x_done(i):
        who = lax.rem(g + 2, XN)
        for d in range(2):
            h = x_part(i, who, d, True)
            rcopy(h, h, xs.at[i, d, 1], xr.at[i, d, 1], si, gr if d == 0 else gl).wait_recv()

    for t in range(10):
        if t < 8:
            y_near(ORDER[t])
            x_start(ORDER[t])
        if 1 <= t < 9:
            y_far(ORDER[t - 1])
            x_fwd(ORDER[t - 1])
        if t >= 2:
            x_done(ORDER[t - 2])
    own.wait()
    for a in range(8):
        for b in range(4):
            s = sid(z + (ZN - a), y + (YN - b), 1 - c)
            rcopy(wall.at[s], wall.at[s], ss.at[a, b], sr.at[a, b], sib, g).wait_recv()
    for cp in sends:
        cp.wait_send()


def vm():
    return pl.BlockSpec(memory_space=pltpu.VMEM)


def fetch(wsh, cache, slot):
    dma = pltpu.SemaphoreType.DMA
    return pl.pallas_call(
        fetch_kernel,
        name="fetch",
        out_shape=(
            jax.ShapeDtypeStruct((64, 4, 16, 576), BF),
            jax.ShapeDtypeStruct((64, 64, 8, 128), BF),
            jax.ShapeDtypeStruct((64, 16, 256), BF),
        ),
        in_specs=[vm()] * 3,
        out_specs=(vm(),) * 3,
        scratch_shapes=[
            pltpu.VMEM((64, 8, 128), jnp.int32),
            pltpu.VMEM((64, 16, 576), BF),
            dma((2, 4)), dma((2, 4)),
            dma((8, 2, 2)), dma((8, 2, 2)),
            dma((8, 4)), dma((8, 4)),
            dma((8, 4, 2)), dma((8, 4, 2)),
            dma((8, 4, 2)), dma((8, 4, 2)),
            dma((8, 2, 2)), dma((8, 2, 2)),
            dma((2,)),
        ],
        compiler_params=pltpu.CompilerParams(has_side_effects=True),
    )(wsh, cache, slot)


def give_kernel(dk, m_ref, out, fl, fr, nl, nr, tol, tor, send, got,
                fs, fr_, ns, nr_, as_, ar, gs, gr_):
    si, g, z, y, c = place()
    gr, gl, go2 = lax.rem(g + 1, XN), lax.rem(g + 3, XN), lax.rem(g + 2, XN)
    sends = []

    def go(cp):
        cp.start()
        sends.append(cp)

    def lo(i):
        return pl.ds(8 * lax.rem(z + i, ZN), 4)

    def hi(i):
        return pl.ds(8 * lax.rem(z + i, ZN) + 4, 4)

    for i in ORDER:
        go(rcopy(dk.at[lo(i), go2], fl.at[i], fs.at[i, 0], fr_.at[i, 0], si, gr))
        go(rcopy(dk.at[hi(i), go2], fr.at[i], fs.at[i, 1], fr_.at[i, 1], si, gl))
        go(rcopy(dk.at[hi(i), gr], nl.at[hi(i)], ns.at[i, 0, 0], nr_.at[i, 0, 0], si, gr))
        go(rcopy(dk.at[lo(i), gl], nr.at[lo(i)], ns.at[i, 1, 0], nr_.at[i, 1, 0], si, gl))

    def combine(i):
        rcopy(fl.at[i], fl.at[i], fs.at[i, 0], fr_.at[i, 0], si, gr).wait_recv()
        tor[i] = (dk[lo(i), gr].astype(F32) + fl[i].astype(F32)).astype(BF)
        rcopy(fr.at[i], fr.at[i], fs.at[i, 1], fr_.at[i, 1], si, gl).wait_recv()
        tol[i] = (dk[hi(i), gl].astype(F32) + fr[i].astype(F32)).astype(BF)
        go(rcopy(tor.at[i], nl.at[lo(i)], ns.at[i, 0, 1], nr_.at[i, 0, 1], si, gr))
        go(rcopy(tol.at[i], nr.at[hi(i)], ns.at[i, 1, 1], nr_.at[i, 1, 1], si, gl))

    def owner(i):
        rcopy(nl.at[hi(i)], nl.at[hi(i)], ns.at[i, 0, 0], nr_.at[i, 0, 0], si, gr).wait_recv()
        rcopy(nr.at[lo(i)], nr.at[lo(i)], ns.at[i, 1, 0], nr_.at[i, 1, 0], si, gl).wait_recv()
        rcopy(nl.at[lo(i)], nl.at[lo(i)], ns.at[i, 0, 1], nr_.at[i, 0, 1], si, gr).wait_recv()
        rcopy(nr.at[hi(i)], nr.at[hi(i)], ns.at[i, 1, 1], nr_.at[i, 1, 1], si, gl).wait_recv()
        al = pl.ds(8 * lax.rem(z + i, ZN), 8)
        send[al] = (dk[al, g].astype(F32) + nl[al].astype(F32) + nr[al].astype(F32)).astype(BF)
        for dy in range(YN):
            for dc in range(2):
                if (i, dy, dc) != (0, 0, 0):
                    to = sid(z + i, y + dy, lax.rem(c + dc, 2))
                    go(rcopy(send.at[to], got.at[si], as_.at[i, dy, dc], ar.at[i, dy, dc], to, g))

    for t in range(9):
        if t < 8:
            combine(ORDER[t])
        if t >= 1:
            owner(ORDER[t - 1])
    got[si] = send[si]
    for (dz, dy, dc) in peers():
        s = sid(z + (ZN - dz), y + (YN - dy), lax.rem(c + dc, 2))
        rcopy(got.at[s], got.at[s], as_.at[dz, dy, dc], ar.at[dz, dy, dc], s, g).wait_recv()
    acc = lax.dot_general(m_ref[...].reshape(1024, 256), got[...].reshape(1024, 576),
                          (((0,), (0,)), ((), ())), preferred_element_type=F32)
    out[:, g] = acc.astype(BF).reshape(16, 16, 576)
    ref = out.at[:, g]
    go(rcopy(ref, ref, gs.at[0, 0], gr_.at[0, 0], si, gr))
    go(rcopy(ref, ref, gs.at[1, 0], gr_.at[1, 0], si, gl))
    for d in range(2):
        who, to = (gl, gr) if d == 0 else (gr, gl)
        ref = out.at[:, who]
        rcopy(ref, ref, gs.at[d, 0], gr_.at[d, 0], si, to).wait_recv()
        h = out.at[pl.ds(8 * d, 8), who]
        go(rcopy(h, h, gs.at[d, 1], gr_.at[d, 1], si, to))
    for d in range(2):
        h = out.at[pl.ds(8 * d, 8), go2]
        rcopy(h, h, gs.at[d, 1], gr_.at[d, 1], si, gr if d == 0 else gl).wait_recv()
    for cp in sends:
        cp.wait_send()


def give(dk, m):
    dma = pltpu.SemaphoreType.DMA
    return pl.pallas_call(
        give_kernel,
        name="give",
        out_shape=jax.ShapeDtypeStruct((16, 4, 16, 576), BF),
        in_specs=[vm()] * 2,
        out_specs=vm(),
        scratch_shapes=[
            pltpu.VMEM((8, 4, 16, 576), BF), pltpu.VMEM((8, 4, 16, 576), BF),
            pltpu.VMEM((64, 16, 576), BF), pltpu.VMEM((64, 16, 576), BF),
            pltpu.VMEM((8, 4, 16, 576), BF), pltpu.VMEM((8, 4, 16, 576), BF),
            pltpu.VMEM((64, 16, 576), BF), pltpu.VMEM((64, 16, 576), BF),
            dma((8, 2)), dma((8, 2)),
            dma((8, 2, 2)), dma((8, 2, 2)),
            dma((8, 4, 2)), dma((8, 4, 2)),
            dma((2, 2)), dma((2, 2)),
        ],
        compiler_params=pltpu.CompilerParams(has_side_effects=True),
    )(dk, m)


NT = (((1,), (1,)), ((), ()))
TN = (((0,), (0,)), ((), ()))
SCALE = 1.0 / math.sqrt(192.0)
TJ = 512


def attend_kernel(qn, qr, do, keys, wall, bias, attn, dqn, dqr, dk,
                  qf, dol, e_ref, dp_ref, mj_ref, dqt, ot, gsum, ol, dql):
    rep = jnp.where(
        lax.broadcasted_iota(jnp.int32, (128, 512), 1) // 4 == lax.broadcasted_iota(jnp.int32, (128, 512), 0), 1.0, 0.0
    ).astype(BF)
    lb_mask = lax.rem(lax.broadcasted_iota(jnp.int32, (64, 512), 1), 4) == (
        lax.broadcasted_iota(jnp.int32, (64, 512), 0) // 16
    )

    def weight(i):
        return wall[:, i].astype(F32).reshape(512, 128).astype(BF)

    def project(h, carry):
        rows = pl.ds(pl.multiple_of(16 * h, 16), 16)
        wide = jnp.dot(qn[h], rep, preferred_element_type=F32)
        wide = jnp.where(lb_mask, jnp.concatenate([wide] * 4, axis=0), 0.0).astype(BF)
        lat = jnp.dot(wide, weight(h), preferred_element_type=F32)
        qf[rows, 0:512] = jnp.concatenate([lat[16 * b:16 * b + 16] for b in range(4)], axis=1).astype(BF)
        dol[rows, :] = lax.dot_general(do[h], weight(32 + h), NT, preferred_element_type=F32).astype(BF)
        return carry

    lax.fori_loop(0, 32, project, 0)
    qf[:, 512:576] = qr[...]

    def first(j, carry):
        m, l, d = carry
        kj = keys[pl.ds(pl.multiple_of(TJ * j, TJ), TJ), :]
        s = lax.dot_general(kj, qf[...], NT, preferred_element_type=F32) * SCALE
        b = bias[pl.ds(pl.multiple_of(8 * j, 8), 8), :]
        s = (s.reshape(8, 64, 512) + b[:, None, :]).reshape(TJ, 512)
        mn = jnp.maximum(m, jnp.max(s, axis=0, keepdims=True))
        e = jnp.exp(s - mn)
        dp = lax.dot_general(kj[:, :512], dol[...], NT, preferred_element_type=F32)
        e_ref[j] = e
        dp_ref[j] = dp
        mj_ref[j] = mn
        al = jnp.exp(m - mn)
        return (mn, l * al + jnp.sum(e, axis=0, keepdims=True), d * al + jnp.sum(e * dp, axis=0, keepdims=True))

    one = jnp.zeros((1, 512), F32)
    m, l, d = lax.fori_loop(0, 8, first, (one + NEG, one, one))
    inv = 1.0 / l
    delta = d * inv
    dqt[...] = jnp.zeros_like(dqt)
    ot[...] = jnp.zeros_like(ot)

    def second(j, carry):
        rows = pl.ds(pl.multiple_of(TJ * j, TJ), TJ)
        kj = keys[rows, :]
        p = e_ref[j] * (jnp.exp(mj_ref[j] - m) * inv)
        pb = p.astype(BF)
        ds = (p * (dp_ref[j] - delta) * SCALE).astype(BF)
        gk = jnp.dot(ds, qf[...], preferred_element_type=F32)
        gv = jnp.dot(pb, dol[...], preferred_element_type=F32)
        dk[rows, 0:512] = (gk[:, :512] + gv).astype(BF)
        dk[rows, 512:576] = gk[:, 512:].astype(BF)
        dqt[...] += lax.dot_general(kj, ds, TN, preferred_element_type=F32)
        ot[...] += lax.dot_general(kj[:, :512], pb, TN, preferred_element_type=F32)
        return carry

    lax.fori_loop(0, 8, second, 0)
    ol[...] = jnp.transpose(ot[...]).astype(BF)
    dql[...] = jnp.transpose(dqt[0:512, :]).astype(BF)
    dqr[...] = jnp.transpose(dqt[512:576, :]).astype(BF)

    def finish(h, carry):
        rows = pl.ds(pl.multiple_of(16 * h, 16), 16)
        attn[h] = jnp.dot(ol[rows, :], weight(32 + h), preferred_element_type=F32).astype(BF)
        x = dql[rows, :]
        x = jnp.concatenate([x[:, 128 * b:128 * b + 128] for b in range(4)], axis=0)
        r = lax.dot_general(x, weight(h), NT, preferred_element_type=F32)
        r = jnp.where(lb_mask, r, 0.0)
        gsum[rows, :] = r[0:16] + r[16:32] + r[32:48] + r[48:64]
        return carry

    lax.fori_loop(0, 32, finish, 0)
    gs = gsum[...]
    g0 = gs.astype(BF)
    r1 = gs - g0.astype(F32)
    g1 = r1.astype(BF)
    g2 = (r1 - g1.astype(F32)).astype(BF)
    acc = lax.dot_general(g0, rep, NT, preferred_element_type=F32)
    acc += lax.dot_general(g1, rep, NT, preferred_element_type=F32)
    acc += lax.dot_general(g2, rep, NT, preferred_element_type=F32)
    dqn[...] = acc.astype(BF)


def attend(qn, qr, do, keys, wall, bias):
    return pl.pallas_call(
        attend_kernel,
        name="attend",
        out_shape=(
            jax.ShapeDtypeStruct((32, 16, 128), BF),
            jax.ShapeDtypeStruct((512, 128), BF),
            jax.ShapeDtypeStruct((512, 64), BF),
            jax.ShapeDtypeStruct((4096, 576), BF),
        ),
        in_specs=[vm()] * 6,
        out_specs=(vm(),) * 4,
        scratch_shapes=[
            pltpu.VMEM((512, 576), BF), pltpu.VMEM((512, 512), BF),
            pltpu.VMEM((8, TJ, 512), F32), pltpu.VMEM((8, TJ, 512), F32),
            pltpu.VMEM((8, 1, 512), F32),
            pltpu.VMEM((576, 512), F32), pltpu.VMEM((512, 512), F32),
            pltpu.VMEM((512, 512), F32), pltpu.VMEM((512, 512), BF), pltpu.VMEM((512, 512), BF),
        ],
        compiler_params=pltpu.CompilerParams(vmem_limit_bytes=62 << 20),
    )(qn, qr, do, keys, wall, bias)


def local(q_nope, q_rope, cache, w_uk, w_uv, d_out, sel, slot_blocks):
    wsh = jnp.concatenate([w_uk.reshape(32, 8, 128), w_uv.reshape(32, 8, 128)], axis=0)
    slot = jnp.pad(jnp.broadcast_to(slot_blocks, (8, 64)), ((0, 0), (0, 64)))
    keys, wall, m = fetch(wsh, cache.reshape(16, 4, 16, 576), slot)
    qn = jnp.transpose(q_nope, (1, 0, 2))
    do = jnp.transpose(d_out, (1, 0, 2))
    qr = jnp.transpose(q_rope, (1, 0, 2)).reshape(512, 64)
    chosen = jnp.any(sel[:, :, None] == jnp.arange(64, dtype=jnp.int32)[None, None, :], axis=1)
    bias = jnp.tile(jnp.where(chosen, 0.0, NEG).astype(F32).T, (1, 32))
    attn, dqn, dqr, dk = attend(qn, qr, do, keys.reshape(4096, 576), wall, bias)
    dc = give(dk.reshape(64, 4, 16, 576), m)
    return (
        jnp.transpose(attn, (1, 0, 2)),
        jnp.transpose(dqn.reshape(32, 16, 128), (1, 0, 2)),
        jnp.transpose(dqr.reshape(32, 16, 64), (1, 0, 2)),
        dc.astype(F32).reshape(1024, 576),
    )


def solution(mesh):
    return jax.shard_map(
        local,
        mesh=mesh,
        in_specs=(
            P("seq", "grp", None),
            P("seq", "grp", None),
            P("seq", None),
            P("grp", "seq"),
            P("grp", "seq"),
            P("seq", "grp", None),
            P("seq", None),
            P("seq", None),
        ),
        out_specs=(
            P("seq", "grp", None),
            P("seq", "grp", None),
            P("seq", "grp", None),
            P("seq", None),
        ),
        check_vma=False,
    )
```

```python
import math

import jax
import jax.numpy as jnp
from jax import lax
from jax.experimental import pallas as pl
from jax.experimental.pallas import tpu as pltpu
from jax.sharding import PartitionSpec as P

MESH = pl.DeviceIdType.MESH
BF = jnp.bfloat16
F32 = jnp.float32
ZN, YN, XN = 8, 4, 4
ORDER = (0, 5, 2, 7, 4, 1, 6, 3)
NEG = -1e30
ORDER_W = (0, 1, 7, 2, 6, 3, 5, 4)


def rcopy(src, dst, ssem, rsem, seq, grp):
    return pltpu.make_async_remote_copy(
        src_ref=src, dst_ref=dst, send_sem=ssem, recv_sem=rsem,
        device_id=(seq, grp), device_id_type=MESH,
    )


def place():
    si = lax.axis_index("seq")
    g = lax.axis_index("grp")
    c = lax.rem(si, 2)
    y = lax.rem(si // 2, YN)
    z = si // (2 * YN)
    return si, g, z, y, c


def sid(z, y, c):
    return (lax.rem(z, ZN) * YN + lax.rem(y, YN)) * 2 + c


def peers():
    return [(dz, dy, dc) for dz in ORDER for dy in range(YN) for dc in range(2) if (dz, dy, dc) != (0, 0, 0)]


NT = (((1,), (1,)), ((), ()))
TN = (((0,), (0,)), ((), ()))
SCALE = 1.0 / math.sqrt(192.0)


def step_of(t):
    return lax.rem(5 * t, 8)


def whole_kernel(qn_in, qr_in, do_in, cache, wk_in, wv_in, sel, slot,
                 attn, dqn, dqr, out,
                 wsh, wall, table, m_ref, send, keys,
                 qn, do, qf, dol, bias, e_ref, dp_ref, mj_ref, dk,
                 dqt, ot, ol, dql, at_t, fl, fr, nl, nr, tol, tor, got,
                 zs, zr, ys, yr, ss, sr, ixs, ixr, as_, ar, xs, xr, loc,
                 fs, fq, ns, nq, bs, br, gs, gq):
    si, g, z, y, c = place()
    zp, zm = sid(z + 1, y, c), sid(z + 7, y, c)
    yp, ym = sid(z, y + 1, c), sid(z, y + 3, c)
    sib = sid(z, y, 1 - c)
    gr, gl, gf = lax.rem(g + 1, XN), lax.rem(g + 3, XN), lax.rem(g + 2, XN)
    barrier = pltpu.get_barrier_semaphore()
    for (dz, dy, dc) in peers():
        pl.semaphore_signal(barrier, inc=1, device_id=(sid(z + dz, y + dy, lax.rem(c + dc, 2)), g), device_id_type=MESH)
    pl.semaphore_signal(barrier, inc=1, device_id=(si, gr), device_id_type=MESH)
    pl.semaphore_signal(barrier, inc=1, device_id=(si, gl), device_id_type=MESH)

    for i, w_in in ((0, wk_in), (32, wv_in)):
        wsh[i:i + 32] = w_in[...].astype(F32).reshape(32, 8, 128).astype(BF)
    pl.semaphore_wait(barrier, 65)

    late = []

    def go(cp):
        cp.start()
        late.append(cp)

    def src_of(a, b):
        return sid(z + (ZN - a), y + (YN - b), c)

    def tiles(ref, kv, h=None):
        if h is None:
            return ref.at[pl.ds(32 * kv, 32)]
        return ref.at[pl.ds(32 * kv + 16 * h, 16)]

    own = pltpu.make_async_copy(wsh, wall.at[si], loc.at[0])
    own.start()
    mine = pltpu.make_async_copy(slot, table.at[si], loc.at[1])
    mine.start()
    go(rcopy(tiles(wsh, 0), tiles(wall.at[si], 0), zs.at[0, 0, 0], zr.at[0, 0, 0], zp, g))
    go(rcopy(tiles(wsh, 0), tiles(wall.at[si], 0), zs.at[0, 1, 0], zr.at[0, 1, 0], zm, g))
    for (dz, dy, dc) in peers():
        to = sid(z + dz, y + dy, lax.rem(c + dc, 2))
        go(rcopy(slot, table.at[si], ixs.at[dz, dy, dc], ixr.at[dz, dy, dc], to, g))
    go(rcopy(tiles(wsh, 1), tiles(wall.at[si], 1), zs.at[1, 0, 0], zr.at[1, 0, 0], zp, g))
    go(rcopy(tiles(wsh, 1), tiles(wall.at[si], 1), zs.at[1, 1, 0], zr.at[1, 1, 0], zm, g))

    def y_send(kv, a):
        s = src_of(a, 0)
        ref = tiles(wsh if a == 0 else wall.at[s], kv)
        dst = tiles(wall.at[s], kv)
        go(rcopy(ref, dst, ys.at[kv, a, 0, 0], yr.at[kv, a, 0, 0], yp, g))
        go(rcopy(ref, dst, ys.at[kv, a, 1, 0], yr.at[kv, a, 1, 0], ym, g))
        go(rcopy(ref, dst, ss.at[kv, a, 0], sr.at[kv, a, 0], sib, g))

    def z_step(kv, k):
        for d in range(2):
            a = k if d == 0 else ZN - k
            s = src_of(a, 0)
            ref = tiles(wall.at[s], kv) if k < 4 else tiles(wall.at[s], kv, d)
            to = zp if d == 0 else zm
            rcopy(ref, ref, zs.at[kv, d, k - 1], zr.at[kv, d, k - 1], to, g).wait_recv()
            if k < 4:
                nxt = tiles(wall.at[s], kv) if k < 3 else tiles(wall.at[s], kv, d)
                go(rcopy(nxt, nxt, zs.at[kv, d, k], zr.at[kv, d, k], to, g))

    def y_near(kv, a):
        for d in range(2):
            b = 1 if d == 0 else 3
            s = src_of(a, b)
            ref = tiles(wall.at[s], kv)
            to = yp if d == 0 else ym
            rcopy(ref, ref, ys.at[kv, a, d, 0], yr.at[kv, a, d, 0], to, g).wait_recv()
            h = tiles(wall.at[s], kv, d)
            go(rcopy(h, h, ys.at[kv, a, d, 1], yr.at[kv, a, d, 1], to, g))
            go(rcopy(ref, ref, ss.at[kv, a, b], sr.at[kv, a, b], sib, g))

    def y_far(kv, a):
        s = src_of(a, 2)
        for d in range(2):
            h = tiles(wall.at[s], kv, d)
            rcopy(h, h, ys.at[kv, a, d, 1], yr.at[kv, a, d, 1], yp if d == 0 else ym, g).wait_recv()
        ref = tiles(wall.at[s], kv)
        go(rcopy(ref, ref, ss.at[kv, a, 2], sr.at[kv, a, 2], sib, g))

    def sib_wait(kv):
        for a in range(8):
            for b in range(4):
                ref = tiles(wall.at[sid(z + (ZN - a), y + (YN - b), 1 - c)], kv)
                rcopy(ref, ref, ss.at[kv, a, b], sr.at[kv, a, b], sib, g).wait_recv()

    y_send(0, 0)
    z_step(0, 1)
    y_send(0, 1)
    y_send(0, 7)
    mine.wait()
    z_step(0, 2)
    y_send(0, 2)
    y_send(0, 6)
    z_step(1, 1)
    z_step(0, 3)
    y_send(0, 3)
    y_send(0, 5)
    z_step(1, 2)
    z_step(0, 4)
    y_send(0, 4)
    z_step(1, 3)
    for (dz, dy, dc) in peers():
        s = sid(z + (ZN - dz), y + (YN - dy), lax.rem(c + dc, 2))
        rcopy(slot, table.at[s], ixs.at[dz, dy, dc], ixr.at[dz, dy, dc], s, g).wait_recv()

    lane = lax.broadcasted_iota(jnp.int32, (1, 64), 1)
    col = lax.broadcasted_iota(jnp.int32, (16, 256), 1)
    row = lax.broadcasted_iota(jnp.int32, (16, 256), 0)
    colb, same = col // 16, lax.rem(col, 16) == row

    def build(i, carry):
        for k in range(8):
            r = 8 * i + k
            v = jnp.sum(jnp.where(lane == si, table[r].astype(F32), 0.0), axis=1, keepdims=True).astype(jnp.int32)
            hit = (colb == jnp.broadcast_to(v, (16, 256))) & same
            m_ref[r] = jnp.where(hit, 1.0, 0.0).astype(BF)
        return carry

    lax.fori_loop(0, 8, build, 0)
    cq = cache[:, g].reshape(256, 576)

    def pick(i, carry):
        rows = pl.ds(8 * i, 8)
        pulled = jnp.dot(m_ref[rows].reshape(128, 256), cq, preferred_element_type=F32)
        send[rows] = pulled.astype(BF).reshape(8, 16, 576)
        return carry

    lax.fori_loop(0, 8, pick, 0)
    keys[si, g] = send[si]
    for (dz, dy, dc) in peers():
        to = sid(z + dz, y + dy, lax.rem(c + dc, 2))
        go(rcopy(send.at[to], keys.at[si, g], as_.at[dz, dy, dc], ar.at[dz, dy, dc], to, g))
    z_step(1, 4)

    qn[...] = jnp.swapaxes(qn_in[...].astype(F32), 0, 1).astype(BF)
    do[...] = jnp.swapaxes(do_in[...].astype(F32), 0, 1).astype(BF)
    qf[:, 512:576] = jnp.swapaxes(qr_in[...].astype(F32), 0, 1).reshape(512, 64).astype(BF)
    chosen = jnp.zeros((16, 64), F32)
    places = lax.broadcasted_iota(jnp.int32, (16, 64), 1)
    picks = sel[...]
    for k in range(32):
        chosen = jnp.where(picks[:, k:k + 1] == places, 1.0, chosen)
    spread = jnp.where(
        lax.rem(lax.broadcasted_iota(jnp.int32, (16, 512), 1), 16) == lax.broadcasted_iota(jnp.int32, (16, 512), 0), 1.0, 0.0
    )
    held = lax.dot_general(chosen.astype(BF), spread.astype(BF), TN, preferred_element_type=F32)
    bias[...] = jnp.where(held > 0.5, 0.0, NEG)

    for t in range(9):
        if t < 8:
            y_near(0, ORDER_W[t])
        if t >= 1:
            y_far(0, ORDER_W[t - 1])
    for t in range(8):
        y_send(1, ORDER_W[t])
    own.wait()

    def x_part(i, who, d=None):
        base = 8 * lax.rem(z + ZN - i, ZN)
        if d is None:
            return keys.at[pl.ds(base, 8), who]
        return keys.at[pl.ds(base + 4 * d, 4), who]

    def x_start(i):
        for dy in range(YN):
            for dc in range(2):
                if (i, dy, dc) != (0, 0, 0):
                    s = sid(z + (ZN - i), y + (YN - dy), lax.rem(c + dc, 2))
                    rcopy(send.at[s], keys.at[s, g], as_.at[i, dy, dc], ar.at[i, dy, dc], s, g).wait_recv()
        ref = x_part(i, g)
        go(rcopy(ref, ref, xs.at[i, 0, 0], xr.at[i, 0, 0], si, gr))
        go(rcopy(ref, ref, xs.at[i, 1, 0], xr.at[i, 1, 0], si, gl))

    def x_fwd(i):
        for d in range(2):
            who, to = (gl, gr) if d == 0 else (gr, gl)
            ref = x_part(i, who)
            rcopy(ref, ref, xs.at[i, d, 0], xr.at[i, d, 0], si, to).wait_recv()
            h = x_part(i, who, d)
            go(rcopy(h, h, xs.at[i, d, 1], xr.at[i, d, 1], si, to))

    def x_done(i):
        for d in range(2):
            h = x_part(i, gf, d)
            rcopy(h, h, xs.at[i, d, 1], xr.at[i, d, 1], si, gr if d == 0 else gl).wait_recv()

    x_start(ORDER[0])
    x_start(ORDER[1])
    x_fwd(ORDER[0])
    sib_wait(0)

    rep = jnp.where(
        lax.broadcasted_iota(jnp.int32, (128, 512), 1) // 4 == lax.broadcasted_iota(jnp.int32, (128, 512), 0), 1.0, 0.0
    ).astype(BF)
    lb_mask = lax.rem(lax.broadcasted_iota(jnp.int32, (64, 512), 1), 4) == (
        lax.broadcasted_iota(jnp.int32, (64, 512), 0) // 16
    )

    def weight(i):
        return wall[:, i].astype(F32).reshape(512, 128).astype(BF)

    def rows16(h):
        return pl.ds(pl.multiple_of(16 * h, 16), 16)

    def project_q(h, carry):
        wide = jnp.dot(qn[h], rep, preferred_element_type=F32)
        wide = jnp.where(lb_mask, jnp.concatenate([wide] * 4, axis=0), 0.0).astype(BF)
        lat = jnp.dot(wide, weight(h), preferred_element_type=F32)
        qf[rows16(h), 0:512] = jnp.concatenate([lat[16 * b:16 * b + 16] for b in range(4)], axis=1).astype(BF)
        return carry

    lax.fori_loop(0, 32, project_q, 0)

    def chunk_keys(zz):
        return keys[pl.ds(8 * zz, 8)].reshape(512, 576)

    def score(i, m, l):
        zz = lax.rem(z + ZN - i, ZN)
        s = lax.dot_general(chunk_keys(zz), qf[...], NT, preferred_element_type=F32) * SCALE
        b = bias[pl.ds(pl.multiple_of(8 * zz, 8), 8), :]
        s = (s.reshape(8, 64, 512) + b[:, None, :]).reshape(512, 512)
        mn = jnp.maximum(m, jnp.max(s, axis=0, keepdims=True))
        e = jnp.exp(s - mn)
        e_ref[zz] = e
        mj_ref[zz] = mn
        return mn, l * jnp.exp(m - mn) + jnp.sum(e, axis=0, keepdims=True)

    zero = jnp.zeros((1, 512), F32)
    m, l = zero + NEG, zero
    for t in range(8):
        y_near(1, ORDER_W[t])
        if t >= 1:
            y_far(1, ORDER_W[t - 1])
        if t < 6:
            x_start(ORDER[t + 2])
        if t < 7:
            x_fwd(ORDER[t + 1])
        x_done(ORDER[t])
        m, l = lax.fori_loop(t, t + 1, lambda k, ml: score(step_of(k), *ml), (m, l))
    y_far(1, ORDER_W[7])
    sib_wait(1)
    inv = 1.0 / l

    def project_d(h, carry):
        dol[rows16(h), :] = lax.dot_general(do[h], weight(32 + h), NT, preferred_element_type=F32).astype(BF)
        return carry

    lax.fori_loop(0, 32, project_d, 0)

    def back(j, d):
        p = e_ref[j] * (jnp.exp(mj_ref[j] - m) * inv)
        dp = lax.dot_general(keys[pl.ds(8 * j, 8)].reshape(512, 576)[:, :512], dol[...], NT, preferred_element_type=F32)
        e_ref[j] = p
        dp_ref[j] = dp
        return d + jnp.sum(p * dp, axis=0, keepdims=True)

    delta = lax.fori_loop(0, 8, back, zero)
    dqt[...] = jnp.zeros_like(dqt)
    ot[...] = jnp.zeros_like(ot)

    def grads(t, carry):
        zz = lax.rem(z + step_of(t + 4), ZN)
        kj = chunk_keys(zz)
        p = e_ref[zz]
        pb = p.astype(BF)
        ds = (p * (dp_ref[zz] - delta) * SCALE).astype(BF)
        gk = jnp.dot(ds, qf[...], preferred_element_type=F32)
        gv = jnp.dot(pb, dol[...], preferred_element_type=F32)
        gk = jnp.concatenate([gk[:, :512] + gv, gk[:, 512:]], axis=1)
        dk[pl.ds(8 * zz, 8)] = gk.astype(BF).reshape(8, 4, 16, 576)
        dqt[...] += lax.dot_general(kj, ds, TN, preferred_element_type=F32)
        ot[...] += lax.dot_general(kj[:, :512], pb, TN, preferred_element_type=F32)
        return carry

    def lo(i):
        return pl.ds(8 * lax.rem(z + i, ZN), 4)

    def hi(i):
        return pl.ds(8 * lax.rem(z + i, ZN) + 4, 4)

    def leave(i):
        go(rcopy(dk.at[lo(i), gf], fl.at[i], fs.at[i, 0], fq.at[i, 0], si, gr))
        go(rcopy(dk.at[hi(i), gf], fr.at[i], fs.at[i, 1], fq.at[i, 1], si, gl))
        go(rcopy(dk.at[hi(i), gr], nl.at[hi(i)], ns.at[i, 0, 0], nq.at[i, 0, 0], si, gr))
        go(rcopy(dk.at[lo(i), gl], nr.at[lo(i)], ns.at[i, 1, 0], nq.at[i, 1, 0], si, gl))

    def combine(i):
        rcopy(fl.at[i], fl.at[i], fs.at[i, 0], fq.at[i, 0], si, gr).wait_recv()
        tor[i] = (dk[lo(i), gr].astype(F32) + fl[i].astype(F32)).astype(BF)
        rcopy(fr.at[i], fr.at[i], fs.at[i, 1], fq.at[i, 1], si, gl).wait_recv()
        tol[i] = (dk[hi(i), gl].astype(F32) + fr[i].astype(F32)).astype(BF)
        go(rcopy(tor.at[i], nl.at[lo(i)], ns.at[i, 0, 1], nq.at[i, 0, 1], si, gr))
        go(rcopy(tol.at[i], nr.at[hi(i)], ns.at[i, 1, 1], nq.at[i, 1, 1], si, gl))

    def owner(i):
        rcopy(nl.at[hi(i)], nl.at[hi(i)], ns.at[i, 0, 0], nq.at[i, 0, 0], si, gr).wait_recv()
        rcopy(nr.at[lo(i)], nr.at[lo(i)], ns.at[i, 1, 0], nq.at[i, 1, 0], si, gl).wait_recv()
        rcopy(nl.at[lo(i)], nl.at[lo(i)], ns.at[i, 0, 1], nq.at[i, 0, 1], si, gr).wait_recv()
        rcopy(nr.at[hi(i)], nr.at[hi(i)], ns.at[i, 1, 1], nq.at[i, 1, 1], si, gl).wait_recv()
        al = pl.ds(8 * lax.rem(z + i, ZN), 8)
        back_send[al] = (dk[al, g].astype(F32) + nl[al].astype(F32) + nr[al].astype(F32)).astype(BF)
        for dy in range(YN):
            for dc in range(2):
                if (i, dy, dc) != (0, 0, 0):
                    to = sid(z + i, y + dy, lax.rem(c + dc, 2))
                    go(rcopy(back_send.at[to], got.at[si], bs.at[i, dy, dc], br.at[i, dy, dc], to, g))

    back_send = at_t
    rorder = [(5 * (t + 4)) % 8 for t in range(8)]
    for t in range(8):
        lax.fori_loop(t, t + 1, grads, 0)
        leave(rorder[t])
        if t >= 2:
            combine(rorder[t - 2])
        if t >= 4:
            owner(rorder[t - 4])
    combine(rorder[6])
    owner(rorder[4])
    ol[...] = jnp.transpose(ot[...]).astype(BF)
    dql[...] = jnp.transpose(dqt[0:512, :]).astype(BF)
    dqr[...] = jnp.swapaxes(jnp.transpose(dqt[512:576, :]).reshape(32, 16, 64), 0, 1).astype(BF)
    combine(rorder[7])
    owner(rorder[5])

    def finish(h, carry):
        qn[h] = jnp.dot(ol[rows16(h), :], weight(32 + h), preferred_element_type=F32).astype(BF)
        x = dql[rows16(h), :]
        x = jnp.concatenate([x[:, 128 * b:128 * b + 128] for b in range(4)], axis=0)
        r = lax.dot_general(x, weight(h), NT, preferred_element_type=F32)
        r = jnp.where(lb_mask, r, 0.0)
        ot[rows16(h), :] = r[0:16] + r[16:32] + r[32:48] + r[48:64]
        return carry

    lax.fori_loop(0, 16, finish, 0)
    owner(rorder[6])
    lax.fori_loop(16, 32, finish, 0)
    owner(rorder[7])
    attn[...] = jnp.swapaxes(qn[...].astype(F32), 0, 1).astype(BF)
    gv0 = ot[...]
    g0 = gv0.astype(BF)
    r1 = gv0 - g0.astype(F32)
    g1 = r1.astype(BF)
    g2 = (r1 - g1.astype(F32)).astype(BF)
    acc = lax.dot_general(g0, rep, NT, preferred_element_type=F32)
    acc += lax.dot_general(g1, rep, NT, preferred_element_type=F32)
    acc += lax.dot_general(g2, rep, NT, preferred_element_type=F32)
    dqn[...] = jnp.swapaxes(acc.reshape(32, 16, 128), 0, 1).astype(BF)

    got[si] = back_send[si]
    for i in rorder:
        for dy in range(YN):
            for dc in range(2):
                if (i, dy, dc) != (0, 0, 0):
                    s = sid(z + (ZN - i), y + (YN - dy), lax.rem(c + dc, 2))
                    rcopy(got.at[s], got.at[s], bs.at[i, dy, dc], br.at[i, dy, dc], s, g).wait_recv()
    total = lax.dot_general(m_ref[...].reshape(1024, 256), got[...].reshape(1024, 576), TN, preferred_element_type=F32)
    out[:, g] = total.astype(BF).reshape(16, 16, 576)
    ref = out.at[:, g]
    go(rcopy(ref, ref, gs.at[0, 0], gq.at[0, 0], si, gr))
    go(rcopy(ref, ref, gs.at[1, 0], gq.at[1, 0], si, gl))
    for d in range(2):
        who, to = (gl, gr) if d == 0 else (gr, gl)
        ref = out.at[:, who]
        rcopy(ref, ref, gs.at[d, 0], gq.at[d, 0], si, to).wait_recv()
        h = out.at[pl.ds(8 * d, 8), who]
        go(rcopy(h, h, gs.at[d, 1], gq.at[d, 1], si, to))
    for d in range(2):
        h = out.at[pl.ds(8 * d, 8), gf]
        rcopy(h, h, gs.at[d, 1], gq.at[d, 1], si, gr if d == 0 else gl).wait_recv()
    for cp in late:
        cp.wait_send()


def vm():
    return pl.BlockSpec(memory_space=pltpu.VMEM)


def whole(*args):
    dma = pltpu.SemaphoreType.DMA
    v = pltpu.VMEM
    half = v((8, 4, 16, 576), BF)
    quarter = v((64, 16, 576), BF)
    return pl.pallas_call(
        whole_kernel,
        name="whole",
        out_shape=(
            jax.ShapeDtypeStruct((16, 32, 128), BF),
            jax.ShapeDtypeStruct((16, 32, 128), BF),
            jax.ShapeDtypeStruct((16, 32, 64), BF),
            jax.ShapeDtypeStruct((16, 4, 16, 576), BF),
        ),
        in_specs=[vm()] * 8,
        out_specs=(vm(),) * 4,
        scratch_shapes=[
            v((64, 8, 128), BF), v((64, 64, 8, 128), BF), v((64, 1, 64), jnp.int32), v((64, 16, 256), BF), quarter,
            v((64, 4, 16, 576), BF),
            v((32, 16, 128), BF), v((32, 16, 128), BF), v((512, 576), BF), v((512, 512), BF), v((64, 512), F32),
            v((8, 512, 512), F32), v((8, 512, 512), F32), v((8, 1, 512), F32), v((64, 4, 16, 576), BF),
            v((576, 512), F32), v((512, 512), F32), v((512, 512), BF), v((512, 512), BF),
            quarter, half, half, quarter, quarter, half, half, quarter,
            dma((2, 2, 4)), dma((2, 2, 4)),
            dma((2, 8, 2, 2)), dma((2, 8, 2, 2)),
            dma((2, 8, 4)), dma((2, 8, 4)),
            dma((8, 4, 2)), dma((8, 4, 2)),
            dma((8, 4, 2)), dma((8, 4, 2)),
            dma((8, 2, 2)), dma((8, 2, 2)),
            dma((2,)),
            dma((8, 2)), dma((8, 2)),
            dma((8, 2, 2)), dma((8, 2, 2)),
            dma((8, 4, 2)), dma((8, 4, 2)),
            dma((2, 2)), dma((2, 2)),
        ],
        compiler_params=pltpu.CompilerParams(has_side_effects=True, collective_id=0, vmem_limit_bytes=67043328),
    )(*args)


def local(q_nope, q_rope, cache, w_uk, w_uv, d_out, sel, slot_blocks):
    attn, dqn, dqr, dc = whole(
        q_nope, q_rope, d_out, cache.reshape(16, 4, 16, 576), w_uk, w_uv, sel, slot_blocks
    )
    return (attn, dqn, dqr, dc.astype(F32).reshape(1024, 576))

def solution(mesh):
    return jax.shard_map(
        local,
        mesh=mesh,
        in_specs=(
            P("seq", "grp", None),
            P("seq", "grp", None),
            P("seq", None),
            P("grp", "seq"),
            P("grp", "seq"),
            P("seq", "grp", None),
            P("seq", None),
            P("seq", None),
        ),
        out_specs=(
            P("seq", "grp", None),
            P("seq", "grp", None),
            P("seq", "grp", None),
            P("seq", None),
        ),
        check_vma=False,
    )
```

```python
import math

import jax
import jax.numpy as jnp
from jax import lax
from jax.experimental import pallas as pl
from jax.experimental.pallas import tpu as pltpu
from jax.sharding import PartitionSpec as P

MESH = pl.DeviceIdType.MESH
BF = jnp.bfloat16
F32 = jnp.float32
ZN, YN, XN = 8, 4, 4
ORDER = (0, 1, 7, 2, 6, 3, 5, 4)
RORDER = (4, 3, 5, 2, 6, 1, 7, 0)
NEG = -1e30


def rcopy(src, dst, ssem, rsem, seq, grp):
    return pltpu.make_async_remote_copy(
        src_ref=src, dst_ref=dst, send_sem=ssem, recv_sem=rsem,
        device_id=(seq, grp), device_id_type=MESH,
    )


def place():
    si = lax.axis_index("seq")
    g = lax.axis_index("grp")
    c = lax.rem(si, 2)
    y = lax.rem(si // 2, YN)
    z = si // (2 * YN)
    return si, g, z, y, c


def sid(z, y, c):
    return (lax.rem(z, ZN) * YN + lax.rem(y, YN)) * 2 + c


def peers():
    return [(dz, dy, dc) for dz in ORDER for dy in range(YN) for dc in range(2) if (dz, dy, dc) != (0, 0, 0)]


NT = (((1,), (1,)), ((), ()))
TN = (((0,), (0,)), ((), ()))
SCALE = 1.0 / math.sqrt(192.0)


def whole_kernel(qn_in, qr_in, do_in, cache, wk_in, wv_in, sel, slot,
                 attn, dqn, dqr, out,
                 wsh, wall, table, m_ref, send, keys,
                 qn, do, qf, dol, bias, e_ref, dp_ref, mj_ref, dk,
                 dqt, ot, ol, dql, at_t, fl, fr, nl, nr, tol, tor, got,
                 sent, zr, yr, yq, sr, ixr, ar, xr, xq, fq, nq, br, gr_, gq, loc):
    si, g, z, y, c = place()
    zp, zm = sid(z + 1, y, c), sid(z + 7, y, c)
    yp, ym = sid(z, y + 1, c), sid(z, y + 3, c)
    sib = sid(z, y, 1 - c)
    gr, gl, gf = lax.rem(g + 1, XN), lax.rem(g + 3, XN), lax.rem(g + 2, XN)
    barrier = pltpu.get_barrier_semaphore()
    for (dz, dy, dc) in peers():
        pl.semaphore_signal(barrier, inc=1, device_id=(sid(z + dz, y + dy, lax.rem(c + dc, 2)), g), device_id_type=MESH)
    pl.semaphore_signal(barrier, inc=1, device_id=(si, gr), device_id_type=MESH)
    pl.semaphore_signal(barrier, inc=1, device_id=(si, gl), device_id_type=MESH)

    for i, w_in in ((0, wk_in), (32, wv_in)):
        wsh[i:i + 32] = w_in[...].astype(F32).reshape(32, 8, 128).astype(BF)
    pl.semaphore_wait(barrier, 65)

    def go(src, dst, kind, rsem, seq, grp):
        rcopy(src, dst, sent.at[kind], rsem, seq, grp).start()

    def here(ref, rsem):
        rcopy(ref, ref, sent.at[0], rsem, sib, g).wait_recv()

    def gone(ref, kind):
        rcopy(ref, ref, sent.at[kind], loc.at[0], sib, g).wait_send()

    def src_of(a, b):
        return sid(z + (ZN - a), y + (YN - b), c)

    def tiles(ref, kv, h=None):
        if h is None:
            return ref.at[pl.ds(32 * kv, 32)]
        return ref.at[pl.ds(32 * kv + 16 * h, 16)]

    own = pltpu.make_async_copy(wsh, wall.at[si], loc.at[0])
    mine = pltpu.make_async_copy(slot, table.at[si], loc.at[1])
    mine.start()
    for (dz, dy, dc) in peers():
        to = sid(z + dz, y + dy, lax.rem(c + dc, 2))
        go(slot, table.at[si], 1, ixr.at[0], to, g)
    for kv in range(2):
        go(tiles(wsh, kv), tiles(wall.at[si], kv), 0, zr.at[kv, 0, 0], zp, g)
        go(tiles(wsh, kv), tiles(wall.at[si], kv), 0, zr.at[kv, 1, 0], zm, g)
    own.start()

    def y_send(kv, a):
        s = src_of(a, 0)
        ref = tiles(wsh if a == 0 else wall.at[s], kv)
        dst = tiles(wall.at[s], kv)
        go(ref, dst, 0, yr.at[kv, a, 0], yp, g)
        go(ref, dst, 0, yr.at[kv, a, 1], ym, g)
        go(ref, dst, 0, sr.at[kv], sib, g)

    def z_step(kv, k):
        for d in range(2):
            a = k if d == 0 else ZN - k
            s = src_of(a, 0)
            here(tiles(wall.at[s], kv) if k < 4 else tiles(wall.at[s], kv, d), zr.at[kv, d, k - 1])
            if k < 4:
                nxt = tiles(wall.at[s], kv) if k < 3 else tiles(wall.at[s], kv, d)
                go(nxt, nxt, 0, zr.at[kv, d, k], zp if d == 0 else zm, g)

    def y_near(kv, a):
        for d in range(2):
            ref = wall.at[src_of(a, 1 if d == 0 else 3)]
            here(tiles(ref, kv), yr.at[kv, a, d])
            go(tiles(ref, kv, d), tiles(ref, kv, d), 0, yq.at[kv, a], yp if d == 0 else ym, g)
            go(tiles(ref, kv), tiles(ref, kv), 0, sr.at[kv], sib, g)

    def y_far(kv, a):
        ref = tiles(wall.at[src_of(a, 2)], kv)
        here(ref, yq.at[kv, a])
        go(ref, ref, 0, sr.at[kv], sib, g)

    def sib_wait(kv):
        here(wall.at[pl.ds(0, 16)], sr.at[kv])

    y_send(0, 0)
    rep = jnp.where(
        lax.broadcasted_iota(jnp.int32, (128, 512), 1) // 4 == lax.broadcasted_iota(jnp.int32, (128, 512), 0), 1.0, 0.0
    ).astype(BF)
    qn[...] = jnp.swapaxes(qn_in[...].astype(F32), 0, 1).astype(BF)
    ol[...] = jnp.dot(qn[...].reshape(512, 128), rep, preferred_element_type=F32).astype(BF)
    z_step(0, 1)
    y_send(0, 1)
    y_send(0, 7)
    mine.wait()
    here(table.at[pl.ds(0, 63)], ixr.at[0])

    lane = lax.broadcasted_iota(jnp.int32, (1, 64), 1)
    col = lax.broadcasted_iota(jnp.int32, (16, 256), 1)
    row = lax.broadcasted_iota(jnp.int32, (16, 256), 0)
    colb, same = col // 16, lax.rem(col, 16) == row

    def build(i, carry):
        for k in range(8):
            r = 8 * i + k
            v = jnp.sum(jnp.where(lane == si, table[r].astype(F32), 0.0), axis=1, keepdims=True).astype(jnp.int32)
            hit = (colb == jnp.broadcast_to(v, (16, 256))) & same
            m_ref[r] = jnp.where(hit, 1.0, 0.0).astype(BF)
        return carry

    lax.fori_loop(0, 8, build, 0)
    cq = cache[:, g].reshape(256, 576)

    def pick(i, carry):
        rows = pl.ds(8 * i, 8)
        pulled = jnp.dot(m_ref[rows].reshape(128, 256), cq, preferred_element_type=F32)
        send[rows] = pulled.astype(BF).reshape(8, 16, 576)
        return carry

    lax.fori_loop(0, 8, pick, 0)
    keys[si, g] = send[si]

    def ask(t):
        i = ORDER[t]
        for dy in range(YN):
            for dc in range(2):
                if (i, dy, dc) != (0, 0, 0):
                    to = sid(z + i, y + dy, lax.rem(c + dc, 2))
                    go(send.at[to], keys.at[si, g], 2, ar.at[i], to, g)

    ask(0)
    z_step(0, 2)
    y_send(0, 2)
    y_send(0, 6)
    z_step(1, 1)
    y_near(0, 0)
    z_step(0, 3)
    y_send(0, 3)
    y_send(0, 5)
    z_step(1, 2)
    ask(1)
    ask(2)
    y_near(0, 1)
    z_step(0, 4)
    y_send(0, 4)
    z_step(1, 3)
    z_step(1, 4)
    ask(3)
    ask(4)
    ask(5)
    ask(6)
    ask(7)
    own.wait()

    do[...] = jnp.swapaxes(do_in[...].astype(F32), 0, 1).astype(BF)
    qf[:, 512:576] = jnp.swapaxes(qr_in[...].astype(F32), 0, 1).reshape(512, 64).astype(BF)
    chosen = jnp.zeros((16, 64), F32)
    places = lax.broadcasted_iota(jnp.int32, (16, 64), 1)
    picks = sel[...]
    for k in range(32):
        chosen = jnp.where(picks[:, k:k + 1] == places, 1.0, chosen)
    spread = jnp.where(
        lax.rem(lax.broadcasted_iota(jnp.int32, (16, 512), 1), 16) == lax.broadcasted_iota(jnp.int32, (16, 512), 0), 1.0, 0.0
    )
    held = lax.dot_general(chosen.astype(BF), spread.astype(BF), TN, preferred_element_type=F32)
    bias[...] = jnp.where(held > 0.5, 0.0, NEG)

    def x_part(i, who, d=None):
        base = 8 * lax.rem(z + ZN - i, ZN)
        if d is None:
            return keys.at[pl.ds(base, 8), who]
        return keys.at[pl.ds(base + 4 * d, 4), who]

    def x_start(i):
        ref = x_part(i, g)
        here(keys.at[pl.ds(0, 7), g] if i == 0 else ref, ar.at[i])
        go(ref, ref, 3, xr.at[i, 0], si, gr)
        go(ref, ref, 3, xr.at[i, 1], si, gl)

    def x_fwd(i):
        for d in range(2):
            who, to = (gl, gr) if d == 0 else (gr, gl)
            here(x_part(i, who), xr.at[i, d])
            go(x_part(i, who, d), x_part(i, who, d), 3, xq.at[i], si, to)

    def x_done(i):
        here(x_part(i, gf), xq.at[i])

    lb_mask = lax.rem(lax.broadcasted_iota(jnp.int32, (64, 512), 1), 4) == (
        lax.broadcasted_iota(jnp.int32, (64, 512), 0) // 16
    )

    def weight(i):
        return wall[:, i].astype(F32).reshape(512, 128).astype(BF)

    def rows16(h):
        return pl.ds(pl.multiple_of(16 * h, 16), 16)

    def project_q(h, carry):
        wide = jnp.where(lb_mask, jnp.concatenate([ol[rows16(h), :].astype(F32)] * 4, axis=0), 0.0).astype(BF)
        lat = jnp.dot(wide, weight(h), preferred_element_type=F32)
        qf[rows16(h), 0:512] = jnp.concatenate([lat[16 * b:16 * b + 16] for b in range(4)], axis=1).astype(BF)
        return carry

    def project_d(h, carry):
        dol[rows16(h), :] = lax.dot_general(do[h], weight(32 + h), NT, preferred_element_type=F32).astype(BF)
        return carry

    def chunk_keys(zz):
        return keys[pl.ds(8 * zz, 8)].reshape(512, 576)

    def score(i, m, l):
        zz = lax.rem(z + ZN - i, ZN)
        s = lax.dot_general(chunk_keys(zz), qf[...], NT, preferred_element_type=F32) * SCALE
        b = bias[pl.ds(pl.multiple_of(8 * zz, 8), 8), :]
        s = (s.reshape(8, 64, 512) + b[:, None, :]).reshape(512, 512)
        mn = jnp.maximum(m, jnp.max(s, axis=0, keepdims=True))
        e = jnp.exp(s - mn)
        e_ref[zz] = e
        mj_ref[zz] = mn
        return mn, l * jnp.exp(m - mn) + jnp.sum(e, axis=0, keepdims=True)

    zero = jnp.zeros((1, 512), F32)
    state = [zero + NEG, zero]

    def yn(kv, t):
        y_near(kv, ORDER[t])

    def yf(kv, t):
        y_far(kv, ORDER[t])

    def ys1(t):
        y_send(1, ORDER[t])

    def sc(t):
        x_done(ORDER[t])
        state[:] = score(ORDER[t], *state)

    def pq(h):
        lax.fori_loop(h, h + 8, project_q, 0, unroll=2)

    def pd(h):
        lax.fori_loop(h, h + 8, project_d, 0, unroll=2)

    def xst(t):
        x_start(ORDER[t])

    def xf(t):
        x_fwd(ORDER[t])

    xst(0)
    yf(0, 0)
    yn(0, 2)
    xf(0)
    xst(1)
    yf(0, 1)
    yn(0, 3)
    xst(2)
    xf(1)
    yn(0, 4)
    yf(0, 2)
    xf(2)
    yn(0, 5)
    yf(0, 3)
    yn(0, 6)
    yf(0, 4)
    xst(3)
    yn(0, 7)
    yf(0, 5)
    ys1(0)
    ys1(1)
    ys1(2)
    ys1(3)
    ys1(4)
    ys1(5)
    ys1(6)
    ys1(7)
    xst(4)
    xf(3)
    yf(0, 6)
    yf(0, 7)
    xf(4)
    sib_wait(0)
    pq(0)
    pq(8)
    yn(1, 0)
    pq(16)
    pq(24)
    sc(0)
    sc(1)
    yn(1, 1)
    yf(1, 0)
    sc(2)
    xst(5)
    yn(1, 2)
    yf(1, 1)
    sc(3)
    xst(6)
    xf(5)
    yn(1, 3)
    yf(1, 2)
    sc(4)
    xf(6)
    yn(1, 4)
    yf(1, 3)
    xst(7)
    yn(1, 5)
    yf(1, 4)
    sc(5)
    yn(1, 6)
    yf(1, 5)
    sc(6)
    yn(1, 7)
    xf(7)
    yf(1, 6)
    yf(1, 7)
    sib_wait(1)
    pd(0)
    pd(8)
    pd(16)
    pd(24)
    sc(7)
    m, l = state
    inv = 1.0 / l

    def back(j, d):
        p = e_ref[j] * (jnp.exp(mj_ref[j] - m) * inv)
        dp = lax.dot_general(keys[pl.ds(8 * j, 8)].reshape(512, 576)[:, :512], dol[...], NT, preferred_element_type=F32)
        e_ref[j] = p
        dp_ref[j] = dp
        return d + jnp.sum(p * dp, axis=0, keepdims=True)

    delta = lax.fori_loop(0, 8, back, zero)
    dqt[...] = jnp.zeros_like(dqt)
    ot[...] = jnp.zeros_like(ot)

    def grads(i):
        zz = lax.rem(z + i, ZN)
        kj = chunk_keys(zz)
        p = e_ref[zz]
        pb = p.astype(BF)
        ds = (p * (dp_ref[zz] - delta) * SCALE).astype(BF)
        gk = jnp.dot(ds, qf[...], preferred_element_type=F32)
        gv = jnp.dot(pb, dol[...], preferred_element_type=F32)
        gk = jnp.concatenate([gk[:, :512] + gv, gk[:, 512:]], axis=1)
        dk[pl.ds(8 * zz, 8)] = gk.astype(BF).reshape(8, 4, 16, 576)
        dqt[...] += lax.dot_general(kj, ds, TN, preferred_element_type=F32)
        ot[...] += lax.dot_general(kj[:, :512], pb, TN, preferred_element_type=F32)

    def lo(i):
        return pl.ds(8 * lax.rem(z + i, ZN), 4)

    def hi(i):
        return pl.ds(8 * lax.rem(z + i, ZN) + 4, 4)

    def leave(i):
        go(dk.at[lo(i), gf], fl.at[i], 4, fq.at[i, 0], si, gr)
        go(dk.at[hi(i), gf], fr.at[i], 4, fq.at[i, 1], si, gl)
        go(dk.at[hi(i), gr], nl.at[hi(i)], 4, nq.at[i], si, gr)
        go(dk.at[lo(i), gl], nr.at[lo(i)], 4, nq.at[i], si, gl)

    def combine(i):
        here(fl.at[i], fq.at[i, 0])
        tor[i] = (dk[lo(i), gr].astype(F32) + fl[i].astype(F32)).astype(BF)
        here(fr.at[i], fq.at[i, 1])
        tol[i] = (dk[hi(i), gl].astype(F32) + fr[i].astype(F32)).astype(BF)
        go(tor.at[i], nl.at[lo(i)], 4, nq.at[i], si, gr)
        go(tol.at[i], nr.at[hi(i)], 4, nq.at[i], si, gl)

    def owner(i):
        here(dk.at[pl.ds(0, 4)], nq.at[i])
        al = pl.ds(8 * lax.rem(z + i, ZN), 8)
        back_send[al] = (dk[al, g].astype(F32) + nl[al].astype(F32) + nr[al].astype(F32)).astype(BF)
        for dy in range(YN):
            for dc in range(2):
                if (i, dy, dc) != (0, 0, 0):
                    to = sid(z + i, y + dy, lax.rem(c + dc, 2))
                    go(back_send.at[to], got.at[si], 5, br.at[0], to, g)

    back_send = at_t
    for t in range(8):
        grads(RORDER[t])
        leave(RORDER[t])
        if t >= 2:
            combine(RORDER[t - 2])
        if t >= 4:
            owner(RORDER[t - 4])
    combine(RORDER[6])
    owner(RORDER[4])
    gone(wall.at[pl.ds(0, 63)], 0)
    gone(table.at[pl.ds(0, 63)], 1)
    gone(send.at[pl.ds(0, 63)], 2)
    gone(keys.at[pl.ds(0, 48)], 3)
    ol[...] = jnp.transpose(ot[...]).astype(BF)
    combine(RORDER[7])
    owner(RORDER[5])
    dql[...] = jnp.transpose(dqt[0:512, :]).astype(BF)
    owner(RORDER[6])
    dqr[...] = jnp.swapaxes(jnp.transpose(dqt[512:576, :]).reshape(32, 16, 64), 0, 1).astype(BF)
    owner(RORDER[7])
    got[si] = back_send[si]

    def finish(h, carry):
        qn[h] = jnp.dot(ol[rows16(h), :], weight(32 + h), preferred_element_type=F32).astype(BF)
        x = dql[rows16(h), :]
        x = jnp.concatenate([x[:, 128 * b:128 * b + 128] for b in range(4)], axis=0)
        r = lax.dot_general(x, weight(h), NT, preferred_element_type=F32)
        r = jnp.where(lb_mask, r, 0.0)
        ot[rows16(h), :] = r[0:16] + r[16:32] + r[32:48] + r[48:64]
        return carry

    lax.fori_loop(0, 32, finish, 0, unroll=2)
    here(got.at[pl.ds(0, 63)], br.at[0])
    total = lax.dot_general(m_ref[...].reshape(1024, 256), got[...].reshape(1024, 576), TN, preferred_element_type=F32)
    out[:, g] = total.astype(BF).reshape(16, 16, 576)
    ref = out.at[:, g]
    go(ref, ref, 6, gr_.at[0], si, gr)
    go(ref, ref, 6, gr_.at[1], si, gl)
    gone(dk.at[pl.ds(0, 48)], 4)
    gone(back_send.at[pl.ds(0, 63)], 5)
    attn[...] = jnp.swapaxes(qn[...].astype(F32), 0, 1).astype(BF)
    gv0 = ot[...]
    g0 = gv0.astype(BF)
    r1 = gv0 - g0.astype(F32)
    g1 = r1.astype(BF)
    g2 = (r1 - g1.astype(F32)).astype(BF)
    acc = lax.dot_general(g0, rep, NT, preferred_element_type=F32)
    acc += lax.dot_general(g1, rep, NT, preferred_element_type=F32)
    acc += lax.dot_general(g2, rep, NT, preferred_element_type=F32)
    dqn[...] = jnp.swapaxes(acc.reshape(32, 16, 128), 0, 1).astype(BF)
    for d in range(2):
        who, to = (gl, gr) if d == 0 else (gr, gl)
        here(out.at[:, who], gr_.at[d])
        h = out.at[pl.ds(8 * d, 8), who]
        go(h, h, 6, gq.at[0], si, to)
    here(out.at[:, gf], gq.at[0])
    gone(out.at[pl.ds(0, 12)], 6)


def vm():
    return pl.BlockSpec(memory_space=pltpu.VMEM)


def whole(*args):
    dma = pltpu.SemaphoreType.DMA
    v = pltpu.VMEM
    half = v((8, 4, 16, 576), BF)
    quarter = v((64, 16, 576), BF)
    return pl.pallas_call(
        whole_kernel,
        name="whole",
        out_shape=(
            jax.ShapeDtypeStruct((16, 32, 128), BF),
            jax.ShapeDtypeStruct((16, 32, 128), BF),
            jax.ShapeDtypeStruct((16, 32, 64), BF),
            jax.ShapeDtypeStruct((16, 4, 16, 576), BF),
        ),
        in_specs=[vm()] * 8,
        out_specs=(vm(),) * 4,
        scratch_shapes=[
            v((64, 8, 128), BF), v((64, 64, 8, 128), BF), v((64, 1, 64), jnp.int32), v((64, 16, 256), BF), quarter,
            v((64, 4, 16, 576), BF),
            v((32, 16, 128), BF), v((32, 16, 128), BF), v((512, 576), BF), v((512, 512), BF), v((64, 512), F32),
            v((8, 512, 512), F32), v((8, 512, 512), F32), v((8, 1, 512), F32), v((64, 4, 16, 576), BF),
            v((576, 512), F32), v((512, 512), F32), v((512, 512), BF), v((512, 512), BF),
            quarter, half, half, quarter, quarter, half, half, quarter,
            dma((7,)), dma((2, 2, 4)), dma((2, 8, 2)), dma((2, 8)), dma((2,)), dma((1,)), dma((8,)),
            dma((8, 2)), dma((8,)), dma((8, 2)), dma((8,)), dma((1,)), dma((2,)), dma((1,)), dma((2,)),
        ],
        compiler_params=pltpu.CompilerParams(has_side_effects=True, collective_id=0, vmem_limit_bytes=67043328),
    )(*args)


def local(q_nope, q_rope, cache, w_uk, w_uv, d_out, sel, slot_blocks):
    attn, dqn, dqr, dc = whole(
        q_nope, q_rope, d_out, cache.reshape(16, 4, 16, 576), w_uk, w_uv, sel, slot_blocks
    )
    return (attn, dqn, dqr, dc.astype(F32).reshape(1024, 576))

def solution(mesh):
    return jax.shard_map(
        local,
        mesh=mesh,
        in_specs=(
            P("seq", "grp", None),
            P("seq", "grp", None),
            P("seq", None),
            P("grp", "seq"),
            P("grp", "seq"),
            P("seq", "grp", None),
            P("seq", None),
            P("seq", None),
        ),
        out_specs=(
            P("seq", "grp", None),
            P("seq", "grp", None),
            P("seq", "grp", None),
            P("seq", None),
        ),
        check_vma=False,
    )
```

```python
import math

import jax
import jax.numpy as jnp
from jax import lax
from jax.experimental import pallas as pl
from jax.experimental.pallas import tpu as pltpu
from jax.sharding import PartitionSpec as P

MESH = pl.DeviceIdType.MESH
BF = jnp.bfloat16
F32 = jnp.float32
ZN, YN, XN = 8, 4, 4
ORDER = (0, 1, 7, 2, 6, 3, 5, 4)
RORDER = (4, 3, 5, 2, 6, 1, 7, 0)
NEG = -1e30


def rcopy(src, dst, ssem, rsem, seq, grp):
    return pltpu.make_async_remote_copy(
        src_ref=src, dst_ref=dst, send_sem=ssem, recv_sem=rsem,
        device_id=(seq, grp), device_id_type=MESH,
    )


def place():
    si = lax.axis_index("seq")
    g = lax.axis_index("grp")
    c = lax.rem(si, 2)
    y = lax.rem(si // 2, YN)
    z = si // (2 * YN)
    return si, g, z, y, c


def sid(z, y, c):
    return (lax.rem(z, ZN) * YN + lax.rem(y, YN)) * 2 + c


def peers():
    return [(dz, dy, dc) for dz in ORDER for dy in range(YN) for dc in range(2) if (dz, dy, dc) != (0, 0, 0)]


NT = (((1,), (1,)), ((), ()))
TN = (((0,), (0,)), ((), ()))
SCALE = 1.0 / math.sqrt(192.0)


def whole_kernel(qn_in, qr_in, do_in, cache, wk_in, wv_in, sel, slot,
                 attn, dqn, dqr, out,
                 wsh, wall, table, m_ref, send, keys,
                 qn, do, qf, dol, bias, e_ref, dp_ref, mj_ref, part, dk,
                 dqt, ot, ol, dql, at_t, fl, fr, nl, nr, tol, tor, got,
                 sent, zr, yr, yq, sr, ixr, ar, xr, xq, fq, nq, br, gr_, gq, loc):
    si, g, z, y, c = place()
    zp, zm = sid(z + 1, y, c), sid(z + 7, y, c)
    yp, ym = sid(z, y + 1, c), sid(z, y + 3, c)
    sib = sid(z, y, 1 - c)
    gr, gl, gf = lax.rem(g + 1, XN), lax.rem(g + 3, XN), lax.rem(g + 2, XN)
    barrier = pltpu.get_barrier_semaphore()
    for (dz, dy, dc) in peers():
        pl.semaphore_signal(barrier, inc=1, device_id=(sid(z + dz, y + dy, lax.rem(c + dc, 2)), g), device_id_type=MESH)
    pl.semaphore_signal(barrier, inc=1, device_id=(si, gr), device_id_type=MESH)
    pl.semaphore_signal(barrier, inc=1, device_id=(si, gl), device_id_type=MESH)

    for i, w_in in ((0, wk_in), (32, wv_in)):
        wsh[i:i + 32] = w_in[...].astype(F32).reshape(32, 8, 128).astype(BF)
    got[...] = jnp.transpose(cache[...]).reshape(64, 16, 576)
    pl.semaphore_wait(barrier, 65)

    def go(src, dst, kind, rsem, seq, grp):
        rcopy(src, dst, sent.at[kind], rsem, seq, grp).start()

    def here(ref, rsem):
        rcopy(ref, ref, sent.at[0], rsem, sib, g).wait_recv()

    def gone(ref, kind):
        rcopy(ref, ref, sent.at[kind], loc.at[0], sib, g).wait_send()

    def src_of(a, b):
        return sid(z + (ZN - a), y + (YN - b), c)

    def tiles(ref, kv, h=None):
        if h is None:
            return ref.at[pl.ds(32 * kv, 32)]
        return ref.at[pl.ds(32 * kv + 16 * h, 16)]

    own = pltpu.make_async_copy(wsh, wall.at[si], loc.at[0])
    mine = pltpu.make_async_copy(slot, table.at[si], loc.at[1])
    mine.start()
    for (dz, dy, dc) in peers():
        to = sid(z + dz, y + dy, lax.rem(c + dc, 2))
        go(slot, table.at[si], 1, ixr.at[0], to, g)
    for kv in range(2):
        go(tiles(wsh, kv), tiles(wall.at[si], kv), 0, zr.at[kv, 0, 0], zp, g)
        go(tiles(wsh, kv), tiles(wall.at[si], kv), 0, zr.at[kv, 1, 0], zm, g)
    own.start()

    def y_send(kv, a):
        s = src_of(a, 0)
        ref = tiles(wsh if a == 0 else wall.at[s], kv)
        dst = tiles(wall.at[s], kv)
        go(ref, dst, 0, yr.at[kv, a, 0], yp, g)
        go(ref, dst, 0, yr.at[kv, a, 1], ym, g)
        go(ref, dst, 0, sr.at[kv], sib, g)

    def z_step(kv, k):
        for d in range(2):
            a = k if d == 0 else ZN - k
            s = src_of(a, 0)
            here(tiles(wall.at[s], kv) if k < 4 else tiles(wall.at[s], kv, d), zr.at[kv, d, k - 1])
            if k < 4:
                nxt = tiles(wall.at[s], kv) if k < 3 else tiles(wall.at[s], kv, d)
                go(nxt, nxt, 0, zr.at[kv, d, k], zp if d == 0 else zm, g)

    def y_near(kv, a):
        for d in range(2):
            ref = wall.at[src_of(a, 1 if d == 0 else 3)]
            here(tiles(ref, kv), yr.at[kv, a, d])
            go(tiles(ref, kv, d), tiles(ref, kv, d), 0, yq.at[kv, a], yp if d == 0 else ym, g)
            go(tiles(ref, kv), tiles(ref, kv), 0, sr.at[kv], sib, g)

    def y_far(kv, a):
        ref = tiles(wall.at[src_of(a, 2)], kv)
        here(ref, yq.at[kv, a])
        go(ref, ref, 0, sr.at[kv], sib, g)

    def sib_wait(kv):
        here(wall.at[pl.ds(0, 16)], sr.at[kv])

    y_send(0, 0)
    rep = jnp.where(
        lax.broadcasted_iota(jnp.int32, (128, 512), 1) // 4 == lax.broadcasted_iota(jnp.int32, (128, 512), 0), 1.0, 0.0
    ).astype(BF)
    qn[...] = jnp.swapaxes(qn_in[...].astype(F32), 0, 1).astype(BF)
    ol[...] = jnp.dot(qn[...].reshape(512, 128), rep, preferred_element_type=F32).astype(BF)
    z_step(0, 1)
    y_near(0, 0)
    y_send(0, 1)
    y_send(0, 7)
    z_step(1, 1)
    mine.wait()
    here(table.at[pl.ds(0, 63)], ixr.at[0])

    lane = lax.broadcasted_iota(jnp.int32, (1, 64), 1)
    col = lax.broadcasted_iota(jnp.int32, (16, 256), 1)
    row = lax.broadcasted_iota(jnp.int32, (16, 256), 0)
    colb, same = col // 16, lax.rem(col, 16) == row

    def build(i, carry):
        for k in range(8):
            r = 8 * i + k
            v = jnp.sum(jnp.where(lane == si, table[r].astype(F32), 0.0), axis=1, keepdims=True).astype(jnp.int32)
            hit = (colb == jnp.broadcast_to(v, (16, 256))) & same
            m_ref[r] = jnp.where(hit, 1.0, 0.0).astype(BF)
        return carry

    lax.fori_loop(0, 8, build, 0)
    cq = jnp.concatenate([got[4 * b + g] for b in range(16)], axis=0)

    def pick(i, carry):
        rows = pl.ds(8 * i, 8)
        pulled = jnp.dot(m_ref[rows].reshape(128, 256), cq, preferred_element_type=F32)
        send[rows] = pulled.astype(BF).reshape(8, 16, 576)
        return carry

    lax.fori_loop(0, 8, pick, 0)
    keys[si, g] = send[si]

    def ask(t):
        i = ORDER[t]
        for dy in range(YN):
            for dc in range(2):
                if (i, dy, dc) != (0, 0, 0):
                    to = sid(z + i, y + dy, lax.rem(c + dc, 2))
                    go(send.at[to], keys.at[si, g], 2, ar.at[i], to, g)

    def x_part(i, who, d=None):
        base = 8 * lax.rem(z + ZN - i, ZN)
        if d is None:
            return keys.at[pl.ds(base, 8), who]
        return keys.at[pl.ds(base + 4 * d, 4), who]

    def x_start(i):
        ref = x_part(i, g)
        here(keys.at[pl.ds(0, 7), g] if i == 0 else ref, ar.at[i])
        go(ref, ref, 3, xr.at[i, 0], si, gr)
        go(ref, ref, 3, xr.at[i, 1], si, gl)

    def x_fwd(i):
        for d in range(2):
            who, to = (gl, gr) if d == 0 else (gr, gl)
            here(x_part(i, who), xr.at[i, d])
            go(x_part(i, who, d), x_part(i, who, d), 3, xq.at[i], si, to)

    def x_done(i):
        here(x_part(i, gf), xq.at[i])

    lb_mask = lax.rem(lax.broadcasted_iota(jnp.int32, (64, 512), 1), 4) == (
        lax.broadcasted_iota(jnp.int32, (64, 512), 0) // 16
    )

    def weight(i):
        return wall[:, i].astype(F32).reshape(512, 128).astype(BF)

    def rows16(h):
        return pl.ds(pl.multiple_of(16 * h, 16), 16)

    def project_q(h, carry):
        wide = jnp.where(lb_mask, jnp.concatenate([ol[rows16(h), :].astype(F32)] * 4, axis=0), 0.0).astype(BF)
        lat = jnp.dot(wide, weight(h), preferred_element_type=F32)
        qf[rows16(h), 0:512] = jnp.concatenate([lat[16 * b:16 * b + 16] for b in range(4)], axis=1).astype(BF)
        return carry

    def project_d(h, carry):
        dol[rows16(h), :] = lax.dot_general(do[h], weight(32 + h), NT, preferred_element_type=F32).astype(BF)
        return carry

    def chunk_keys(zz):
        return keys[pl.ds(8 * zz, 8)].reshape(512, 576)

    def score(i, m, l):
        zz = lax.rem(z + ZN - i, ZN)
        s = lax.dot_general(chunk_keys(zz), qf[...], NT, preferred_element_type=F32) * SCALE
        b = bias[pl.ds(pl.multiple_of(8 * zz, 8), 8), :]
        s = (s.reshape(8, 64, 512) + b[:, None, :]).reshape(512, 512)
        mn = jnp.maximum(m, jnp.max(s, axis=0, keepdims=True))
        e = jnp.exp(s - mn)
        e_ref[zz] = e
        mj_ref[zz] = mn
        return mn, l * jnp.exp(m - mn) + jnp.sum(e, axis=0, keepdims=True)

    zero = jnp.zeros((1, 512), F32)
    state = [zero + NEG, zero]

    def yn(kv, t):
        y_near(kv, ORDER[t])

    def yf(kv, t):
        y_far(kv, ORDER[t])

    def ys(kv, t):
        y_send(kv, ORDER[t])

    def sc(t):
        x_done(ORDER[t])
        state[:] = score(ORDER[t], *state)

    def dps(t):
        zz = lax.rem(z + ZN - ORDER[t], ZN)
        dp = lax.dot_general(chunk_keys(zz)[:, :512], dol[...], NT, preferred_element_type=F32)
        dp_ref[zz] = dp
        part[zz] = jnp.sum(e_ref[zz] * dp, axis=0, keepdims=True)

    def pq(h):
        lax.fori_loop(h, h + 8, project_q, 0, unroll=2)

    def pd(h):
        lax.fori_loop(h, h + 8, project_d, 0, unroll=2)

    def xst(t):
        x_start(ORDER[t])

    def xf(t):
        x_fwd(ORDER[t])

    z_step(0, 2)
    yn(0, 1)
    ys(0, 3)
    ys(0, 4)
    yf(0, 0)
    z_step(1, 2)
    ask(0)
    yn(0, 2)
    yf(0, 1)
    z_step(0, 3)
    ys(0, 5)
    ys(0, 6)
    ask(1)
    ask(2)
    yn(0, 3)
    z_step(1, 3)
    z_step(0, 4)
    yn(0, 4)
    ys(0, 7)
    ask(3)
    ask(4)
    ask(5)
    ask(6)
    ask(7)
    own.wait()

    do[...] = jnp.swapaxes(do_in[...].astype(F32), 0, 1).astype(BF)
    qf[:, 512:576] = jnp.swapaxes(qr_in[...].astype(F32), 0, 1).reshape(512, 64).astype(BF)
    chosen = jnp.zeros((16, 64), F32)
    places = lax.broadcasted_iota(jnp.int32, (16, 64), 1)
    picks = sel[...]
    for k in range(32):
        chosen = jnp.where(picks[:, k:k + 1] == places, 1.0, chosen)
    spread = jnp.where(
        lax.rem(lax.broadcasted_iota(jnp.int32, (16, 512), 1), 16) == lax.broadcasted_iota(jnp.int32, (16, 512), 0), 1.0, 0.0
    )
    held = lax.dot_general(chosen.astype(BF), spread.astype(BF), TN, preferred_element_type=F32)
    bias[...] = jnp.where(held > 0.5, 0.0, NEG)
    xst(0)
    yf(0, 2)
    yn(0, 5)
    yn(0, 6)
    xf(0)
    xst(1)
    yf(0, 3)
    yf(0, 4)
    xst(2)
    z_step(1, 4)
    yn(0, 7)
    ys(1, 0)
    ys(1, 1)
    ys(1, 2)
    ys(1, 3)
    ys(1, 4)
    ys(1, 5)
    ys(1, 6)
    ys(1, 7)
    xf(1)
    xf(2)
    xst(3)
    xst(4)
    yf(0, 5)
    yf(0, 6)
    yf(0, 7)
    xf(3)
    sib_wait(0)
    pq(0)
    yn(1, 0)
    pq(8)
    pq(16)
    yn(1, 1)
    xf(4)
    pq(24)
    yn(1, 2)
    sc(0)
    sc(1)
    yn(1, 3)
    sc(2)
    xst(5)
    sc(3)
    yn(1, 4)
    xst(6)
    sc(4)
    yn(1, 5)
    yn(1, 6)
    yn(1, 7)
    yf(1, 0)
    yf(1, 1)
    yf(1, 2)
    yf(1, 3)
    xf(5)
    yf(1, 4)
    xst(7)
    yf(1, 5)
    xf(6)
    yf(1, 6)
    yf(1, 7)
    sc(5)
    sib_wait(1)
    pd(0)
    pd(8)
    pd(16)
    pd(24)
    xf(7)
    dps(0)
    dps(1)
    dps(2)
    dps(3)
    dps(4)
    dps(5)
    sc(6)
    dps(6)
    sc(7)
    dps(7)
    m, l = state
    inv = 1.0 / l

    delta = zero
    for i in range(8):
        delta += jnp.exp(mj_ref[i] - m) * part[i]
    delta = delta * inv
    dqt[...] = jnp.zeros_like(dqt)
    ot[...] = jnp.zeros_like(ot)

    def grads(i):
        zz = lax.rem(z + i, ZN)
        kj = chunk_keys(zz)
        p = e_ref[zz] * (jnp.exp(mj_ref[zz] - m) * inv)
        pb = p.astype(BF)
        ds = (p * (dp_ref[zz] - delta) * SCALE).astype(BF)
        gk = jnp.dot(ds, qf[...], preferred_element_type=F32)
        gv = jnp.dot(pb, dol[...], preferred_element_type=F32)
        gk = jnp.concatenate([gk[:, :512] + gv, gk[:, 512:]], axis=1)
        dk[pl.ds(8 * zz, 8)] = gk.astype(BF).reshape(8, 4, 16, 576)
        dqt[...] += lax.dot_general(kj, ds, TN, preferred_element_type=F32)
        ot[...] += lax.dot_general(kj[:, :512], pb, TN, preferred_element_type=F32)

    def lo(i):
        return pl.ds(8 * lax.rem(z + i, ZN), 4)

    def hi(i):
        return pl.ds(8 * lax.rem(z + i, ZN) + 4, 4)

    def leave(i):
        go(dk.at[lo(i), gf], fl.at[i], 4, fq.at[i, 0], si, gr)
        go(dk.at[hi(i), gf], fr.at[i], 4, fq.at[i, 1], si, gl)
        go(dk.at[hi(i), gr], nl.at[hi(i)], 4, nq.at[i], si, gr)
        go(dk.at[lo(i), gl], nr.at[lo(i)], 4, nq.at[i], si, gl)

    def combine(i):
        here(fl.at[i], fq.at[i, 0])
        tor[i] = (dk[lo(i), gr].astype(F32) + fl[i].astype(F32)).astype(BF)
        here(fr.at[i], fq.at[i, 1])
        tol[i] = (dk[hi(i), gl].astype(F32) + fr[i].astype(F32)).astype(BF)
        go(tor.at[i], nl.at[lo(i)], 4, nq.at[i], si, gr)
        go(tol.at[i], nr.at[hi(i)], 4, nq.at[i], si, gl)

    def owner(i):
        here(dk.at[pl.ds(0, 4)], nq.at[i])
        al = pl.ds(8 * lax.rem(z + i, ZN), 8)
        back_send[al] = (dk[al, g].astype(F32) + nl[al].astype(F32) + nr[al].astype(F32)).astype(BF)
        for dy in range(YN):
            for dc in range(2):
                if (i, dy, dc) != (0, 0, 0):
                    to = sid(z + i, y + dy, lax.rem(c + dc, 2))
                    go(back_send.at[to], got.at[si], 5, br.at[0], to, g)

    back_send = at_t
    for t in range(8):
        grads(RORDER[t])
        leave(RORDER[t])
        if t >= 2:
            combine(RORDER[t - 2])
        if t >= 4:
            owner(RORDER[t - 4])
    combine(RORDER[6])
    owner(RORDER[4])
    gone(wall.at[pl.ds(0, 63)], 0)
    gone(table.at[pl.ds(0, 63)], 1)
    gone(send.at[pl.ds(0, 63)], 2)
    gone(keys.at[pl.ds(0, 48)], 3)
    ol[...] = jnp.transpose(ot[...]).astype(BF)
    combine(RORDER[7])
    owner(RORDER[5])
    dql[...] = jnp.transpose(dqt[0:512, :]).astype(BF)
    owner(RORDER[6])
    dqr[...] = jnp.swapaxes(jnp.transpose(dqt[512:576, :]).reshape(32, 16, 64), 0, 1).astype(BF)
    owner(RORDER[7])
    got[si] = back_send[si]

    def finish(h, carry):
        qn[h] = jnp.dot(ol[rows16(h), :], weight(32 + h), preferred_element_type=F32).astype(BF)
        x = dql[rows16(h), :]
        x = jnp.concatenate([x[:, 128 * b:128 * b + 128] for b in range(4)], axis=0)
        r = lax.dot_general(x, weight(h), NT, preferred_element_type=F32)
        r = jnp.where(lb_mask, r, 0.0)
        ot[rows16(h), :] = r[0:16] + r[16:32] + r[32:48] + r[48:64]
        return carry

    lax.fori_loop(0, 32, finish, 0, unroll=2)
    here(got.at[pl.ds(0, 63)], br.at[0])
    total = lax.dot_general(m_ref[...].reshape(1024, 256), got[...].reshape(1024, 576), TN, preferred_element_type=F32)
    out[:, g] = total.astype(BF).reshape(16, 16, 576)
    ref = out.at[:, g]
    go(ref, ref, 6, gr_.at[0], si, gr)
    go(ref, ref, 6, gr_.at[1], si, gl)
    gone(dk.at[pl.ds(0, 48)], 4)
    gone(back_send.at[pl.ds(0, 63)], 5)
    attn[...] = jnp.swapaxes(qn[...].astype(F32), 0, 1).astype(BF)
    gv0 = ot[...]
    g0 = gv0.astype(BF)
    r1 = gv0 - g0.astype(F32)
    g1 = r1.astype(BF)
    g2 = (r1 - g1.astype(F32)).astype(BF)
    acc = lax.dot_general(g0, rep, NT, preferred_element_type=F32)
    acc += lax.dot_general(g1, rep, NT, preferred_element_type=F32)
    acc += lax.dot_general(g2, rep, NT, preferred_element_type=F32)
    dqn[...] = jnp.swapaxes(acc.reshape(32, 16, 128), 0, 1).astype(BF)
    for d in range(2):
        who, to = (gl, gr) if d == 0 else (gr, gl)
        here(out.at[:, who], gr_.at[d])
        h = out.at[pl.ds(8 * d, 8), who]
        go(h, h, 6, gq.at[0], si, to)
    here(out.at[:, gf], gq.at[0])
    gone(out.at[pl.ds(0, 12)], 6)


def vm():
    return pl.BlockSpec(memory_space=pltpu.VMEM)


def whole(*args):
    dma = pltpu.SemaphoreType.DMA
    v = pltpu.VMEM
    half = v((8, 4, 16, 576), BF)
    quarter = v((64, 16, 576), BF)
    return pl.pallas_call(
        whole_kernel,
        name="whole",
        out_shape=(
            jax.ShapeDtypeStruct((16, 32, 128), BF),
            jax.ShapeDtypeStruct((16, 32, 128), BF),
            jax.ShapeDtypeStruct((16, 32, 64), BF),
            jax.ShapeDtypeStruct((16, 4, 16, 576), BF),
        ),
        in_specs=[vm()] * 8,
        out_specs=(vm(),) * 4,
        scratch_shapes=[
            v((64, 8, 128), BF), v((64, 64, 8, 128), BF), v((64, 1, 64), jnp.int32), v((64, 16, 256), BF), quarter,
            v((64, 4, 16, 576), BF),
            v((32, 16, 128), BF), v((32, 16, 128), BF), v((512, 576), BF), v((512, 512), BF), v((64, 512), F32),
            v((8, 512, 512), F32), v((8, 512, 512), F32), v((8, 1, 512), F32), v((8, 1, 512), F32), v((64, 4, 16, 576), BF),
            v((576, 512), F32), v((512, 512), F32), v((512, 512), BF), v((512, 512), BF),
            quarter, half, half, quarter, quarter, half, half, quarter,
            dma((7,)), dma((2, 2, 4)), dma((2, 8, 2)), dma((2, 8)), dma((2,)), dma((1,)), dma((8,)),
            dma((8, 2)), dma((8,)), dma((8, 2)), dma((8,)), dma((1,)), dma((2,)), dma((1,)), dma((2,)),
        ],
        compiler_params=pltpu.CompilerParams(has_side_effects=True, collective_id=0, vmem_limit_bytes=67043328),
    )(*args)


def local(q_nope, q_rope, cache, w_uk, w_uv, d_out, sel, slot_blocks):
    attn, dqn, dqr, dc = whole(
        q_nope, q_rope, d_out, cache.T, w_uk, w_uv, sel, slot_blocks
    )
    return (attn, dqn, dqr, dc.astype(F32).reshape(1024, 576))

def solution(mesh):
    return jax.shard_map(
        local,
        mesh=mesh,
        in_specs=(
            P("seq", "grp", None),
            P("seq", "grp", None),
            P("seq", None),
            P("grp", "seq"),
            P("grp", "seq"),
            P("seq", "grp", None),
            P("seq", None),
            P("seq", None),
        ),
        out_specs=(
            P("seq", "grp", None),
            P("seq", "grp", None),
            P("seq", "grp", None),
            P("seq", None),
        ),
        check_vma=False,
    )
```

```python
import math

import jax
import jax.numpy as jnp
from jax import lax
from jax.experimental import pallas as pl
from jax.experimental.pallas import tpu as pltpu
from jax.sharding import PartitionSpec as P

MESH = pl.DeviceIdType.MESH
BF = jnp.bfloat16
F32 = jnp.float32
ZN, YN, XN = 8, 4, 4
ORDER = (0, 1, 7, 2, 6, 3, 5, 4)
RORDER = (4, 3, 5, 2, 6, 1, 7, 0)
NEG = -1e30


def rcopy(src, dst, ssem, rsem, seq, grp):
    return pltpu.make_async_remote_copy(
        src_ref=src, dst_ref=dst, send_sem=ssem, recv_sem=rsem,
        device_id=(seq, grp), device_id_type=MESH,
    )


def place():
    si = lax.axis_index("seq")
    g = lax.axis_index("grp")
    c = lax.rem(si, 2)
    y = lax.rem(si // 2, YN)
    z = si // (2 * YN)
    return si, g, z, y, c


def sid(z, y, c):
    return (lax.rem(z, ZN) * YN + lax.rem(y, YN)) * 2 + c


def peers():
    return [(dz, dy, dc) for dz in ORDER for dy in range(YN) for dc in range(2) if (dz, dy, dc) != (0, 0, 0)]


NT = (((1,), (1,)), ((), ()))
TN = (((0,), (0,)), ((), ()))
SCALE = 1.0 / math.sqrt(192.0)


def whole_kernel(qn_in, qr_in, do_in, cache, wk_in, wv_in, sel, slot,
                 attn, dqn, dqr, flip0, flip1,
                 wsh, wall, table, m_ref, send, keys,
                 qn, do, qf, dol, bias, e_ref, dp_ref, mj_ref, part,
                 dqt, ot, ol, dql, cs, dk0, dk1, dk2, fl0, fl1, fl2, fr0, fr1, fr2,
                 nl0, nl1, nl2, nr0, nr1, nr2, tl0, tl1, tl2, tr0, tr1, tr2, bs0, bs1, got0, got1, out0, out1,
                 sent, zr, yr, yq, sr, ixr, ar, xr, xq, fq, nq, br, gr_, gq, loc):
    si, g, z, y, c = place()
    zp, zm = sid(z + 1, y, c), sid(z + 7, y, c)
    yp, ym = sid(z, y + 1, c), sid(z, y + 3, c)
    sib = sid(z, y, 1 - c)
    gr, gl, gf = lax.rem(g + 1, XN), lax.rem(g + 3, XN), lax.rem(g + 2, XN)
    barrier = pltpu.get_barrier_semaphore()
    for (dz, dy, dc) in peers():
        pl.semaphore_signal(barrier, inc=1, device_id=(sid(z + dz, y + dy, lax.rem(c + dc, 2)), g), device_id_type=MESH)
    pl.semaphore_signal(barrier, inc=1, device_id=(si, gr), device_id_type=MESH)
    pl.semaphore_signal(barrier, inc=1, device_id=(si, gl), device_id_type=MESH)

    for i, w_in in ((0, wk_in), (32, wv_in)):
        wsh[i:i + 32] = w_in[...].astype(F32).reshape(32, 8, 128).astype(BF)
    cs[...] = jnp.transpose(cache[...]).reshape(64, 16, 576)
    pl.semaphore_wait(barrier, 65)

    def go(src, dst, kind, rsem, seq, grp):
        rcopy(src, dst, sent.at[kind], rsem, seq, grp).start()

    def here(ref, rsem):
        rcopy(ref, ref, sent.at[0], rsem, sib, g).wait_recv()

    def gone(ref, kind):
        rcopy(ref, ref, sent.at[kind], loc.at[0], sib, g).wait_send()

    def src_of(a, b):
        return sid(z + (ZN - a), y + (YN - b), c)

    def tiles(ref, kv, h=None):
        if h is None:
            return ref.at[pl.ds(32 * kv, 32)]
        return ref.at[pl.ds(32 * kv + 16 * h, 16)]

    own = pltpu.make_async_copy(wsh, wall.at[si], loc.at[0])
    mine = pltpu.make_async_copy(slot, table.at[si], loc.at[1])
    mine.start()
    for (dz, dy, dc) in peers():
        to = sid(z + dz, y + dy, lax.rem(c + dc, 2))
        go(slot, table.at[si], 1, ixr.at[0], to, g)
    for kv in range(2):
        go(tiles(wsh, kv), tiles(wall.at[si], kv), 0, zr.at[kv, 0, 0], zp, g)
        go(tiles(wsh, kv), tiles(wall.at[si], kv), 0, zr.at[kv, 1, 0], zm, g)
    own.start()

    def y_send(kv, a):
        s = src_of(a, 0)
        ref = tiles(wsh if a == 0 else wall.at[s], kv)
        dst = tiles(wall.at[s], kv)
        go(ref, dst, 0, yr.at[kv, a, 0], yp, g)
        go(ref, dst, 0, yr.at[kv, a, 1], ym, g)
        go(ref, dst, 0, sr.at[kv], sib, g)

    def z_step(kv, k):
        for d in range(2):
            a = k if d == 0 else ZN - k
            s = src_of(a, 0)
            here(tiles(wall.at[s], kv) if k < 4 else tiles(wall.at[s], kv, d), zr.at[kv, d, k - 1])
            if k < 4:
                nxt = tiles(wall.at[s], kv) if k < 3 else tiles(wall.at[s], kv, d)
                go(nxt, nxt, 0, zr.at[kv, d, k], zp if d == 0 else zm, g)

    def y_near(kv, a):
        for d in range(2):
            ref = wall.at[src_of(a, 1 if d == 0 else 3)]
            here(tiles(ref, kv), yr.at[kv, a, d])
            go(tiles(ref, kv, d), tiles(ref, kv, d), 0, yq.at[kv, a], yp if d == 0 else ym, g)
            go(tiles(ref, kv), tiles(ref, kv), 0, sr.at[kv], sib, g)

    def y_far(kv, a):
        ref = tiles(wall.at[src_of(a, 2)], kv)
        here(ref, yq.at[kv, a])
        go(ref, ref, 0, sr.at[kv], sib, g)

    def sib_wait(kv):
        here(wall.at[pl.ds(0, 16)], sr.at[kv])

    y_send(0, 0)
    rep = jnp.where(
        lax.broadcasted_iota(jnp.int32, (128, 512), 1) // 4 == lax.broadcasted_iota(jnp.int32, (128, 512), 0), 1.0, 0.0
    ).astype(BF)
    qn[...] = jnp.swapaxes(qn_in[...].astype(F32), 0, 1).astype(BF)
    ol[...] = jnp.dot(qn[...].reshape(512, 128), rep, preferred_element_type=F32).astype(BF)
    z_step(0, 1)
    y_near(0, 0)
    y_send(0, 1)
    y_send(0, 7)
    z_step(1, 1)
    mine.wait()
    here(table.at[pl.ds(0, 63)], ixr.at[0])

    lane = lax.broadcasted_iota(jnp.int32, (1, 64), 1)
    col = lax.broadcasted_iota(jnp.int32, (16, 256), 1)
    row = lax.broadcasted_iota(jnp.int32, (16, 256), 0)
    colb, same = col // 16, lax.rem(col, 16) == row

    def build(i, carry):
        for k in range(8):
            r = 8 * i + k
            v = jnp.sum(jnp.where(lane == si, table[r].astype(F32), 0.0), axis=1, keepdims=True).astype(jnp.int32)
            hit = (colb == jnp.broadcast_to(v, (16, 256))) & same
            m_ref[r] = jnp.where(hit, 1.0, 0.0).astype(BF)
        return carry

    lax.fori_loop(0, 8, build, 0)
    cq = jnp.concatenate([cs[4 * b + g] for b in range(16)], axis=0)

    def pick(i, carry):
        rows = pl.ds(8 * i, 8)
        pulled = jnp.dot(m_ref[rows].reshape(128, 256), cq, preferred_element_type=F32)
        send[rows] = pulled.astype(BF).reshape(8, 16, 576)
        return carry

    lax.fori_loop(0, 8, pick, 0)
    keys[si, g] = send[si]

    def ask(t):
        i = ORDER[t]
        for dy in range(YN):
            for dc in range(2):
                if (i, dy, dc) != (0, 0, 0):
                    to = sid(z + i, y + dy, lax.rem(c + dc, 2))
                    go(send.at[to], keys.at[si, g], 2, ar.at[i], to, g)

    def x_part(i, who, d=None):
        base = 8 * lax.rem(z + ZN - i, ZN)
        if d is None:
            return keys.at[pl.ds(base, 8), who]
        return keys.at[pl.ds(base + 4 * d, 4), who]

    def x_start(i):
        ref = x_part(i, g)
        here(keys.at[pl.ds(0, 7), g] if i == 0 else ref, ar.at[i])
        go(ref, ref, 3, xr.at[i, 0], si, gr)
        go(ref, ref, 3, xr.at[i, 1], si, gl)

    def x_fwd(i):
        for d in range(2):
            who, to = (gl, gr) if d == 0 else (gr, gl)
            here(x_part(i, who), xr.at[i, d])
            go(x_part(i, who, d), x_part(i, who, d), 3, xq.at[i], si, to)

    def x_done(i):
        here(x_part(i, gf), xq.at[i])

    lb_mask = lax.rem(lax.broadcasted_iota(jnp.int32, (64, 512), 1), 4) == (
        lax.broadcasted_iota(jnp.int32, (64, 512), 0) // 16
    )

    def weight(i):
        return wall[:, i].astype(F32).reshape(512, 128).astype(BF)

    def rows16(h):
        return pl.ds(pl.multiple_of(16 * h, 16), 16)

    def project_q(h, carry):
        wide = jnp.where(lb_mask, jnp.concatenate([ol[rows16(h), :].astype(F32)] * 4, axis=0), 0.0).astype(BF)
        lat = jnp.dot(wide, weight(h), preferred_element_type=F32)
        qf[rows16(h), 0:512] = jnp.concatenate([lat[16 * b:16 * b + 16] for b in range(4)], axis=1).astype(BF)
        return carry

    def project_d(h, carry):
        dol[rows16(h), :] = lax.dot_general(do[h], weight(32 + h), NT, preferred_element_type=F32).astype(BF)
        return carry

    def chunk_keys(zz):
        return keys[pl.ds(8 * zz, 8)].reshape(512, 576)

    def score(i, m, l):
        zz = lax.rem(z + ZN - i, ZN)
        s = lax.dot_general(chunk_keys(zz), qf[...], NT, preferred_element_type=F32) * SCALE
        b = bias[pl.ds(pl.multiple_of(8 * zz, 8), 8), :]
        s = (s.reshape(8, 64, 512) + b[:, None, :]).reshape(512, 512)
        mn = jnp.maximum(m, jnp.max(s, axis=0, keepdims=True))
        e = jnp.exp(s - mn)
        e_ref[zz] = e
        mj_ref[zz] = mn
        return mn, l * jnp.exp(m - mn) + jnp.sum(e, axis=0, keepdims=True)

    zero = jnp.zeros((1, 512), F32)
    state = [zero + NEG, zero]

    def yn(kv, t):
        y_near(kv, ORDER[t])

    def yf(kv, t):
        y_far(kv, ORDER[t])

    def ys(kv, t):
        y_send(kv, ORDER[t])

    def sc(t):
        x_done(ORDER[t])
        state[:] = score(ORDER[t], *state)

    def dps(t):
        zz = lax.rem(z + ZN - ORDER[t], ZN)
        dp = lax.dot_general(chunk_keys(zz)[:, :512], dol[...], NT, preferred_element_type=F32)
        dp_ref[zz] = dp
        part[zz] = jnp.sum(e_ref[zz] * dp, axis=0, keepdims=True)

    def pq(h):
        lax.fori_loop(h, h + 8, project_q, 0, unroll=2)

    def xst(t):
        x_start(ORDER[t])

    def xf(t):
        x_fwd(ORDER[t])

    z_step(0, 2)
    yn(0, 1)
    ys(0, 3)
    ys(0, 4)
    yf(0, 0)
    z_step(1, 2)
    ask(0)
    yn(0, 2)
    yf(0, 1)
    z_step(0, 3)
    ys(0, 5)
    ys(0, 6)
    ask(1)
    ask(2)
    yn(0, 3)
    z_step(1, 3)
    z_step(0, 4)
    yn(0, 4)
    ys(0, 7)
    ask(3)
    ask(4)
    ask(5)
    ask(6)
    ask(7)
    own.wait()

    do[...] = jnp.swapaxes(do_in[...].astype(F32), 0, 1).astype(BF)
    qf[:, 512:576] = jnp.swapaxes(qr_in[...].astype(F32), 0, 1).reshape(512, 64).astype(BF)
    chosen = jnp.zeros((16, 64), F32)
    places = lax.broadcasted_iota(jnp.int32, (16, 64), 1)
    picks = sel[...]
    for k in range(32):
        chosen = jnp.where(picks[:, k:k + 1] == places, 1.0, chosen)
    spread = jnp.where(
        lax.rem(lax.broadcasted_iota(jnp.int32, (16, 512), 1), 16) == lax.broadcasted_iota(jnp.int32, (16, 512), 0), 1.0, 0.0
    )
    held = lax.dot_general(chosen.astype(BF), spread.astype(BF), TN, preferred_element_type=F32)
    bias[...] = jnp.where(held > 0.5, 0.0, NEG)
    xst(0)
    yf(0, 2)
    yn(0, 5)
    yn(0, 6)
    xf(0)
    xst(1)
    yf(0, 3)
    yf(0, 4)
    xst(2)
    z_step(1, 4)
    yn(0, 7)
    ys(1, 0)
    ys(1, 1)
    ys(1, 2)
    ys(1, 3)
    ys(1, 4)
    ys(1, 5)
    ys(1, 6)
    ys(1, 7)
    xf(1)
    xf(2)
    xst(3)
    xst(4)
    yf(0, 5)
    yf(0, 6)
    yf(0, 7)
    xf(3)
    sib_wait(0)
    pq(0)
    yn(1, 0)
    pq(8)
    pq(16)
    yn(1, 1)
    xf(4)
    pq(24)
    yn(1, 2)
    sc(0)
    sc(1)
    yn(1, 3)
    sc(2)
    xst(5)
    sc(3)
    yn(1, 4)
    xst(6)
    sc(4)
    yn(1, 5)
    yn(1, 6)
    yn(1, 7)
    yf(1, 0)
    yf(1, 1)
    yf(1, 2)
    yf(1, 3)
    xf(5)
    yf(1, 4)
    xst(7)
    yf(1, 5)
    xf(6)
    yf(1, 6)
    yf(1, 7)
    sc(5)
    sib_wait(1)
    lax.fori_loop(0, 32, project_d, 0, unroll=4)
    xf(7)
    dps(0)
    dps(1)
    dps(2)
    dps(3)
    dps(4)
    dps(5)
    sc(6)
    dps(6)
    sc(7)
    dps(7)
    m, l = state
    inv = 1.0 / l

    delta = zero
    for i in range(8):
        delta += jnp.exp(mj_ref[i] - m) * part[i]
    delta = delta * inv
    dqt[...] = jnp.zeros_like(dqt)
    ot[...] = jnp.zeros_like(ot)

    def grads(i):
        zz = lax.rem(z + i, ZN)
        kj = chunk_keys(zz)
        p = e_ref[zz] * (jnp.exp(mj_ref[zz] - m) * inv)
        pb = p.astype(BF)
        ds = (p * (dp_ref[zz] - delta) * SCALE).astype(BF)
        gk = jnp.dot(ds, qf[...], preferred_element_type=F32)
        gv = jnp.dot(pb, dol[...], preferred_element_type=F32)
        gr8 = pl.ds(8 * zz, 8)
        dk0[gr8] = (gk[:, :256] + gv[:, :256]).astype(BF).reshape(8, 4, 16, 256)
        dk1[gr8] = (gk[:, 256:512] + gv[:, 256:]).astype(BF).reshape(8, 4, 16, 256)
        pair = gk[:, 512:].reshape(4, 2, 64, 64)
        pair = jnp.concatenate([pair[:, 0], pair[:, 1]], axis=2)
        dk2[pl.ds(4 * zz, 4)] = pair.astype(BF).reshape(4, 4, 16, 128)
        dqt[...] += lax.dot_general(kj, ds, TN, preferred_element_type=F32)
        ot[...] += lax.dot_general(kj[:, :512], pb, TN, preferred_element_type=F32)

    dks, fls, frs = (dk0, dk1, dk2), (fl0, fl1, fl2), (fr0, fr1, fr2)
    nls, nrs, tls, trs = (nl0, nl1, nl2), (nr0, nr1, nr2), (tl0, tl1, tl2), (tr0, tr1, tr2)
    parts = ((1, 2), (0,))
    backs, gots, outs = (bs1, bs0), (got1, got0), (out1, out0)

    def span(i, k, h):
        n = 2 if k == 2 else 4
        return pl.ds(2 * n * lax.rem(z + i, ZN) + n * h, n)

    def leave(p, t):
        i = RORDER[t]
        for k in parts[p]:
            lo, hi = span(i, k, 0), span(i, k, 1)
            go(dks[k].at[lo, gf], fls[k].at[i], 4 + k, fq.at[k, i, 0], si, gr)
            go(dks[k].at[hi, gf], frs[k].at[i], 4 + k, fq.at[k, i, 1], si, gl)
            go(dks[k].at[hi, gr], nls[k].at[hi], 4 + k, nq.at[k, i], si, gr)
            go(dks[k].at[lo, gl], nrs[k].at[lo], 4 + k, nq.at[k, i], si, gl)

    def combine(p, t):
        i = RORDER[t]
        for k in parts[p]:
            lo, hi = span(i, k, 0), span(i, k, 1)
            here(fls[k].at[i], fq.at[k, i, 0])
            trs[k][i] = (dks[k][lo, gr].astype(F32) + fls[k][i].astype(F32)).astype(BF)
            here(frs[k].at[i], fq.at[k, i, 1])
            tls[k][i] = (dks[k][hi, gl].astype(F32) + frs[k][i].astype(F32)).astype(BF)
            go(trs[k].at[i], nls[k].at[lo], 4 + k, nq.at[k, i], si, gr)
            go(tls[k].at[i], nrs[k].at[hi], 4 + k, nq.at[k, i], si, gl)

    def total_of(i, k):
        n = 4 if k == 2 else 8
        here(dks[k].at[pl.ds(0, n // 2)], nq.at[k, i])
        al = pl.ds(n * lax.rem(z + i, ZN), n)
        return dks[k][al, g].astype(F32) + nls[k][al].astype(F32) + nrs[k][al].astype(F32)

    def owner(p, t):
        i = RORDER[t]
        al = pl.ds(8 * lax.rem(z + i, ZN), 8)
        if p == 1:
            bs0[al] = total_of(i, 0).astype(BF)
        else:
            pair = total_of(i, 2)
            pair = jnp.stack([pair[:, :, :64], pair[:, :, 64:]], axis=1).reshape(8, 16, 64)
            bs1[al] = jnp.concatenate([total_of(i, 1), pair], axis=2).astype(BF)
        for dy in range(YN):
            for dc in range(2):
                if (i, dy, dc) != (0, 0, 0):
                    to = sid(z + i, y + dy, lax.rem(c + dc, 2))
                    go(backs[p].at[to], gots[p].at[si], 7 + p, br.at[p], to, g)

    def share(p):
        gots[p][si] = backs[p][si]
        here(gots[p].at[pl.ds(0, 63)], br.at[p])
        w = 320 if p == 0 else 256
        total = lax.dot_general(
            m_ref[...].reshape(1024, 256), gots[p][...].reshape(1024, w), TN, preferred_element_type=F32
        )
        outs[p][:, g] = total.astype(BF).reshape(16, 16, w)
        for h in range(2):
            for d in range(2):
                ref = outs[p].at[pl.ds(8 * (h ^ d), 8), g]
                go(ref, ref, 9 + p, gr_.at[p, d, h], si, gr if d == 0 else gl)

    def pass_on(p):
        for d in range(2):
            who, to = (gl, gr) if d == 0 else (gr, gl)
            h = outs[p].at[pl.ds(8 * d, 8), who]
            here(h, gr_.at[p, d, 0])
            go(h, h, 9 + p, gq.at[p], si, to)

    def near_rest(p):
        for d in range(2):
            here(outs[p].at[pl.ds(8 - 8 * d, 8), gl if d == 0 else gr], gr_.at[p, d, 1])

    for t in range(8):
        grads(RORDER[t])
        leave(0, t)
        if t >= 3:
            combine(0, t - 3)
        if t >= 5:
            owner(0, t - 5)
    leave(1, 0)
    combine(0, 5)
    owner(0, 3)
    leave(1, 1)
    combine(0, 6)
    owner(0, 4)
    leave(1, 2)
    combine(0, 7)
    owner(0, 5)
    combine(1, 0)
    leave(1, 3)
    owner(0, 6)
    combine(1, 1)
    owner(0, 7)
    leave(1, 4)
    owner(1, 0)
    combine(1, 2)
    leave(1, 5)
    gone(wall.at[pl.ds(0, 63)], 0)
    gone(table.at[pl.ds(0, 63)], 1)
    gone(send.at[pl.ds(0, 63)], 2)
    gone(keys.at[pl.ds(0, 48)], 3)
    owner(1, 1)
    combine(1, 3)
    leave(1, 6)
    owner(1, 2)
    share(0)
    combine(1, 4)
    leave(1, 7)
    owner(1, 3)
    combine(1, 5)
    ol[...] = jnp.transpose(ot[...]).astype(BF)
    dql[...] = jnp.transpose(dqt[0:512, :]).astype(BF)
    dqr[...] = jnp.swapaxes(jnp.transpose(dqt[512:576, :]).reshape(32, 16, 64), 0, 1).astype(BF)

    def finish(h, carry):
        qn[h] = jnp.dot(ol[rows16(h), :], weight(32 + h), preferred_element_type=F32).astype(BF)
        x = dql[rows16(h), :]
        x = jnp.concatenate([x[:, 128 * b:128 * b + 128] for b in range(4)], axis=0)
        r = lax.dot_general(x, weight(h), NT, preferred_element_type=F32)
        r = jnp.where(lb_mask, r, 0.0)
        ot[rows16(h), :] = r[0:16] + r[16:32] + r[32:48] + r[48:64]
        return carry

    lax.fori_loop(0, 32, finish, 0, unroll=2)
    owner(1, 4)
    pass_on(0)
    combine(1, 6)
    owner(1, 5)
    combine(1, 7)
    owner(1, 6)
    owner(1, 7)

    share(1)
    near_rest(0)
    here(outs[0].at[:, gf], gq.at[0])
    flip1[...] = jnp.transpose(out1[...].reshape(1024, 320))
    for k, n in ((0, 48), (1, 48), (2, 24)):
        gone(dks[k].at[pl.ds(0, n)], 4 + k)
    for p in range(2):
        gone(backs[p].at[pl.ds(0, 63)], 7 + p)
    attn[...] = jnp.swapaxes(qn[...].astype(F32), 0, 1).astype(BF)
    gv0 = ot[...]
    g0 = gv0.astype(BF)
    r1 = gv0 - g0.astype(F32)
    g1 = r1.astype(BF)
    g2 = (r1 - g1.astype(F32)).astype(BF)
    acc = lax.dot_general(g0, rep, NT, preferred_element_type=F32)
    acc += lax.dot_general(g1, rep, NT, preferred_element_type=F32)
    acc += lax.dot_general(g2, rep, NT, preferred_element_type=F32)
    dqn[...] = jnp.swapaxes(acc.reshape(32, 16, 128), 0, 1).astype(BF)
    pass_on(1)
    near_rest(1)
    here(outs[1].at[:, gf], gq.at[1])
    flip0[...] = jnp.transpose(out0[...].reshape(1024, 256))
    for p in range(2):
        gone(outs[p].at[pl.ds(0, 12)], 9 + p)


def vm():
    return pl.BlockSpec(memory_space=pltpu.VMEM)


def whole(*args):
    dma = pltpu.SemaphoreType.DMA
    v = pltpu.VMEM
    quarter = v((64, 16, 576), BF)
    two = (v((8, 4, 16, 256), BF), v((8, 4, 16, 256), BF), v((8, 2, 16, 128), BF))
    all3 = (v((64, 16, 256), BF), v((64, 16, 256), BF), v((32, 16, 128), BF))
    return pl.pallas_call(
        whole_kernel,
        name="whole",
        out_shape=(
            jax.ShapeDtypeStruct((16, 32, 128), BF),
            jax.ShapeDtypeStruct((16, 32, 128), BF),
            jax.ShapeDtypeStruct((16, 32, 64), BF),
            jax.ShapeDtypeStruct((256, 1024), BF),
            jax.ShapeDtypeStruct((320, 1024), BF),
        ),
        in_specs=[vm()] * 8,
        out_specs=(vm(),) * 5,
        scratch_shapes=[
            v((64, 8, 128), BF), v((64, 64, 8, 128), BF), v((64, 1, 64), jnp.int32), v((64, 16, 256), BF), quarter,
            v((64, 4, 16, 576), BF),
            v((32, 16, 128), BF), v((32, 16, 128), BF), v((512, 576), BF), v((512, 512), BF), v((64, 512), F32),
            v((8, 512, 512), F32), v((8, 512, 512), F32), v((8, 1, 512), F32), v((8, 1, 512), F32),
            v((576, 512), F32), v((512, 512), F32), v((512, 512), BF), v((512, 512), BF), quarter,
            v((64, 4, 16, 256), BF), v((64, 4, 16, 256), BF), v((32, 4, 16, 128), BF),
            *two, *two, *all3, *all3, *two, *two,
            v((64, 16, 256), BF), v((64, 16, 320), BF), v((64, 16, 256), BF), v((64, 16, 320), BF),
            v((16, 4, 16, 256), BF), v((16, 4, 16, 320), BF),
            dma((11,)), dma((2, 2, 4)), dma((2, 8, 2)), dma((2, 8)), dma((2,)), dma((1,)), dma((8,)),
            dma((8, 2)), dma((8,)), dma((3, 8, 2)), dma((3, 8)), dma((2,)), dma((2, 2, 2)), dma((2,)), dma((2,)),
        ],
        compiler_params=pltpu.CompilerParams(has_side_effects=True, collective_id=0, vmem_limit_bytes=67043328),
    )(*args)


def local(q_nope, q_rope, cache, w_uk, w_uv, d_out, sel, slot_blocks):
    attn, dqn, dqr, dc0, dc1 = whole(
        q_nope, q_rope, d_out, cache.T, w_uk, w_uv, sel, slot_blocks
    )
    dc = jnp.concatenate([dc0, dc1], axis=0).astype(F32)
    return (attn, dqn, dqr, dc.T)

def solution(mesh):
    return jax.shard_map(
        local,
        mesh=mesh,
        in_specs=(
            P("seq", "grp", None),
            P("seq", "grp", None),
            P("seq", None),
            P("grp", "seq"),
            P("grp", "seq"),
            P("seq", "grp", None),
            P("seq", None),
            P("seq", None),
        ),
        out_specs=(
            P("seq", "grp", None),
            P("seq", "grp", None),
            P("seq", "grp", None),
            P("seq", None),
        ),
        check_vma=False,
    )
```
